128 devices in a mesh: row: 8 (over y, core), col: 16 (over x, z).
Axes of the slice: x: 4, y: 4, z: 4, core: 2. Of those that a mesh axis runs over, the one named last changes fastest.
Arguments:
- prolong: bfloat16 [12288, 4096], P('col', 'row'), may hold values from -0.21875 to 0.21875
- applied: bfloat16 [12288, 4096], P('row', 'col'), may hold values from -6 to 6
- prolong_pattern: int32 [96, 32], P('col', 'row'), may hold values from 0 to 1, as said below
- applied_pattern: int32 [96, 32], P('row', 'col'), may hold values from 0 to 1, as said below
Outputs:
- coarse_operator: float32 [4096, 4096], P('row', 'col')
The draws below stay inside these ranges and needn't reach their ends.
Inputs may be any that keep to these rules, and one draw needn't show every extreme that they name: In each fine tile row a, the nonzero tiles of prolong_pattern are one run of 1 to 3 consecutive coarse tiles that holds tile a * 32 // 96 (cut at the ends of the range), and the tile (a * 32 // 96 + 32 // 2) mod 32. In each fine tile row a, the nonzero tiles of applied_pattern are one run of 3 to 5 consecutive coarse tiles that holds tile a * 32 // 96 (cut at the ends of the range), and the tile (a * 32 // 96 + 32 // 2) mod 32.
All inputs are finite; a program needn't handle non-finite values.
Results may differ from the reference program's by a relative error of at most 0.0003.
Values may be sent and summed in bfloat16 or wider, within the bound.
A program may use at most 64 MiB of HBM per device.

```python
import jax
import jax.numpy as jnp
from jax import lax

TILE = 128
NCT = 32
NFT = 96
NC = 4096
NF = 12288


def band_pattern(key, reach_low, reach_high):
    first_key, second_key = jax.random.split(key)
    fine_rows = jnp.arange(NFT, dtype=jnp.int32)
    centre = fine_rows * NCT // NFT
    lower_reach = jax.random.randint(first_key, (NFT,), reach_low, reach_high, dtype=jnp.int32)
    upper_reach = jax.random.randint(second_key, (NFT,), reach_low, reach_high, dtype=jnp.int32)
    columns = jnp.arange(NCT, dtype=jnp.int32)[None, :]
    offset = columns - centre[:, None]
    inside = (offset >= -lower_reach[:, None]) & (offset <= upper_reach[:, None])
    far_tile = (centre + NCT // 2) % NCT
    inside = inside | (columns == far_tile[:, None])
    return jnp.where(inside, 1, 0).astype(jnp.int32)


def draw_prolong_pattern(key, part):
    return band_pattern(jax.random.fold_in(key, 11), 0, 2)


def draw_applied_pattern(key, part):
    return band_pattern(jax.random.fold_in(key, 23), 1, 3)


def levels(rng, shape, cuts, least, largest):
    factor_of = 1.0
    for position, blocks in cuts:
        draws = jax.random.uniform(jax.random.fold_in(jax.random.fold_in(rng, 6), position), (blocks,), jnp.float32, least / len(cuts), largest / len(cuts))
        factor_of = factor_of * jnp.repeat(jnp.exp(draws), shape[position] // blocks).reshape((-1,) + (1,) * (len(shape) - 1 - position))
    return factor_of


def bell_draw(own_key, shape, deviation, limit, cuts=(), kind=jnp.bfloat16):
    entries = jax.random.normal(own_key, shape, jnp.float32) * deviation
    if len(cuts) > 0:
        entries = levels(own_key, shape, cuts, -0.22, 0.18) * entries
    return jnp.clip(entries, min=-limit, max=limit).astype(kind)


def setup_inputs(seed: int = 0) -> dict:
    arg_keys = jax.random.split(jax.random.key(seed), 5)
    return {
        "prolong": bell_draw(arg_keys[0], (NF, NC), (2 * TILE * NFT // NCT) ** -0.5, 0.21875, ((0, 16), (1, 8))),
        "applied": bell_draw(arg_keys[1], (NF, NC), 1.0, 6.0, ((0, 8), (1, 16))),
        "prolong_pattern": draw_prolong_pattern(jax.random.fold_in(arg_keys[4], 71), 0),
        "applied_pattern": draw_applied_pattern(jax.random.fold_in(arg_keys[4], 71), 0),
    }


def apply_pattern(matrix, pattern):
    height, width = matrix.shape
    tile_rows, tile_cols = pattern.shape
    weights = pattern.astype(matrix.dtype)
    shaped = matrix.reshape(tile_rows, height // tile_rows, tile_cols, width // tile_cols)
    return (shaped * weights[:, None, :, None]).reshape(height, width)


def reference(prolong, applied, prolong_pattern, applied_pattern):
    masked_p = apply_pattern(prolong, prolong_pattern)
    masked_ap = apply_pattern(applied, applied_pattern)
    return lax.dot_general(masked_p, masked_ap, (((0,), (0,)), ((), ())), preferred_element_type=jnp.float32)
```

```python
import jax
import jax.numpy as jnp
from jax import lax
from jax.experimental import pallas as pl
from jax.experimental.pallas import tpu as pltpu
from jax.sharding import PartitionSpec as P

MESH = pl.DeviceIdType.MESH
TILE = 128
ROWS = 8
COLS = 16
SECTION = 768
HALF = 256
FAR = 5
OWN = 2
SLOTS = 6


def offset_source(c, slot):
    if slot == FAR:
        return (c + 8) % COLS, c >= 0
    cp = c + (slot - 2)
    return cp, jnp.logical_and(cp >= 0, cp < COLS)


def offset_target(cp, slot):
    if slot == FAR:
        return (cp + 8) % COLS, cp >= 0
    c = cp - (slot - 2)
    return c, jnp.logical_and(c >= 0, c < COLS)


def halves(r, cp):
    m, h = cp // 2, cp % 2
    main = m == r
    side0 = jnp.logical_and(m == r + 1, h == 0)
    side1 = jnp.logical_and(m == r - 1, h == 1)
    far = m == (r + 4) % ROWS
    t0 = main | side1 | (far & (h == 0))
    t1 = main | side0 | (far & (h == 1))
    return t0, t1


def kernel(p_hbm, ap_hbm, pp_ref, app_ref, out_ref, pbuf, apbuf, load_sem, psend, precv, apsend, aprecv):
    r = lax.axis_index("row")
    c = lax.axis_index("col")
    own_t = halves(r, c)
    own_any = own_t[0] | own_t[1]

    facts = []
    for slot in range(SLOTS):
        cp, ok = offset_source(c, slot)
        t0, t1 = halves(r, cp)
        facts.append((cp, ok & t0, ok & t1))

    ap_sends = []
    for h in range(2):
        cp = 2 * r + h
        ds = cp - c
        near = (ds >= -2) & (ds <= 2)
        far = (cp % COLS) == (c + 8) % COLS
        there = jnp.where(far, FAR, jnp.clip(ds + 2, 0, 4))
        wanted = near | far
        side = r - 1 if h == 0 else r + 1
        side_ok = (side >= 0) if h == 0 else (side < ROWS)
        ap_sends.append((h, 0, wanted & side_ok, side, there))
        ap_sends.append((h, 1, wanted, (r + 4) % ROWS, there))

    barrier = pltpu.get_barrier_semaphore()
    expected = jnp.int32(0)
    for slot in range(SLOTS):
        cp, t0, t1 = facts[slot]
        live = t0 | t1
        if slot != OWN:
            @pl.when(live)
            def _():
                pl.semaphore_signal(barrier, inc=1, device_id=(r, cp), device_id_type=MESH)
            _, ok = offset_target(c, slot)
            expected = expected + jnp.where(ok & own_any, 1, 0)

        @pl.when(live & (cp // 2 != r))
        def _():
            pl.semaphore_signal(barrier, inc=1, device_id=(cp // 2, c), device_id_type=MESH)
    for _, _, ok, _, _ in ap_sends:
        expected = expected + jnp.where(ok, 1, 0)

    loads = [
        pltpu.make_async_copy(p_hbm.at[:, pl.ds(t * HALF, HALF)], pbuf.at[OWN, t], load_sem.at[t])
        for t in range(2)
    ] + [
        pltpu.make_async_copy(ap_hbm.at[pl.ds(h * SECTION, SECTION), :], apbuf.at[h], load_sem.at[2 + h])
        for h in range(2)
    ]
    for load in loads:
        load.start()
    out_ref[...] = jnp.zeros_like(out_ref)
    for load in loads:
        load.wait()
    for a in range(6):
        rows = pl.ds(a * TILE, TILE)
        for i in range(4):
            lanes = pl.ds(i % 2 * TILE, TILE)
            weight = pp_ref[i, a].astype(jnp.float32).astype(jnp.bfloat16)
            pbuf[OWN, i // 2, rows, lanes] = pbuf[OWN, i // 2, rows, lanes] * weight
    for a in range(12):
        rows = pl.ds(a % 6 * TILE, TILE)
        for j in range(2):
            lanes = pl.ds(j * TILE, TILE)
            weight = app_ref[j, a].astype(jnp.float32).astype(jnp.bfloat16)
            apbuf[a // 6, rows, lanes] = apbuf[a // 6, rows, lanes] * weight

    def p_copy(slot, t, target):
        return pltpu.make_async_remote_copy(
            src_ref=pbuf.at[OWN, t],
            dst_ref=pbuf.at[slot, t],
            send_sem=psend.at[slot, t],
            recv_sem=precv.at[slot, t],
            device_id=(r, target),
            device_id_type=MESH,
        )

    def ap_copy(h, which, row, there):
        return pltpu.make_async_remote_copy(
            src_ref=apbuf.at[h],
            dst_ref=apbuf.at[2 + there],
            send_sem=apsend.at[h, which],
            recv_sem=aprecv.at[there],
            device_id=(row, c),
            device_id_type=MESH,
        )

    @pl.when(expected > 0)
    def _():
        pl.semaphore_wait(barrier, expected)

    for slot in (FAR, 0, 4, 1, 3):
        target, ok = offset_target(c, slot)
        for t in range(2):
            @pl.when(ok & own_t[t])
            def _():
                p_copy(slot, t, target).start()
    for h, which, ok, row, there in ap_sends:
        @pl.when(ok)
        def _():
            ap_copy(h, which, row, there).start()

    for slot in (OWN, 1, 3, 0, 4, FAR):
        cp, t0, t1 = facts[slot]
        m, h = cp // 2, cp % 2
        remote_ap = m != r
        live = t0 | t1

        @pl.when(live & remote_ap)
        def _():
            ap_copy(0, 0, r, slot).wait_recv()

        ap_index = jnp.where(remote_ap, 2 + slot, jnp.where(h == 1, 1, 0))
        for t, present in ((0, t0), (1, t1)):
            @pl.when(present)
            def _():
                if slot != OWN:
                    p_copy(slot, t, c).wait_recv()
                rows = pl.ds(t * HALF, HALF)
                out_ref[rows, :] += lax.dot_general(
                    pbuf[slot, t], apbuf[ap_index], (((0,), (0,)), ((), ())),
                    preferred_element_type=jnp.float32,
                )

    for slot in (FAR, 0, 4, 1, 3):
        target, ok = offset_target(c, slot)
        for t in range(2):
            @pl.when(ok & own_t[t])
            def _():
                p_copy(slot, t, target).wait_send()
    for h, which, ok, row, there in ap_sends:
        @pl.when(ok)
        def _():
            ap_copy(h, which, row, there).wait_send()


def on_device(prolong, applied, prolong_pattern, applied_pattern):
    return pl.pallas_call(
        kernel,
        out_shape=jax.ShapeDtypeStruct((prolong.shape[1], applied.shape[1]), jnp.float32),
        in_specs=[
            pl.BlockSpec(memory_space=pltpu.HBM),
            pl.BlockSpec(memory_space=pltpu.HBM),
            pl.BlockSpec(memory_space=pltpu.SMEM),
            pl.BlockSpec(memory_space=pltpu.SMEM),
        ],
        out_specs=pl.BlockSpec(memory_space=pltpu.VMEM),
        scratch_shapes=[
            pltpu.VMEM((SLOTS, 2, SECTION, HALF), jnp.bfloat16),
            pltpu.VMEM((2 + SLOTS, SECTION, HALF), jnp.bfloat16),
            pltpu.SemaphoreType.DMA((4,)),
            pltpu.SemaphoreType.DMA((SLOTS, 2)),
            pltpu.SemaphoreType.DMA((SLOTS, 2)),
            pltpu.SemaphoreType.DMA((2, 2)),
            pltpu.SemaphoreType.DMA((SLOTS,)),
        ],
        compiler_params=pltpu.CompilerParams(
            collective_id=0, has_side_effects=True, vmem_limit_bytes=63 * 1024 * 1024
        ),
    )(prolong, applied, prolong_pattern.T, applied_pattern.T)


def solution(mesh):
    in_specs = (P("col", "row"), P("row", "col"), P("col", "row"), P("row", "col"))
    out_specs = P("row", "col")
    return jax.shard_map(
        on_device, mesh=mesh, in_specs=in_specs, out_specs=out_specs, check_vma=False
    )
```

```python
import jax
import jax.numpy as jnp
from jax import lax
from jax.experimental import pallas as pl
from jax.experimental.pallas import tpu as pltpu
from jax.sharding import PartitionSpec as P

MESH = pl.DeviceIdType.MESH
TILE = 128
ROWS = 8
COLS = 16
GROUP = 384
HALF = 256
FAR = 5
OWN = 2
SLOTS = 6
RELAYED = 8


def column_of(c, slot):
    near = c + slot - 2
    far = slot == FAR
    cp = jnp.where(far, (c + 8) % COLS, near)
    return cp, far | ((near >= 0) & (near < COLS))


def shape_of(r, cp):
    m, h = cp // 2, cp % 2
    main = m == r
    low = (m == r + 1) & (h == 0)
    high = (m == r - 1) & (h == 1)
    far = m == (r + 4) % ROWS
    any3 = main | low | high | far
    half3 = jnp.where(far, h, 1 - h)
    start3 = jnp.where(main, 1 - h, jnp.where(high, 1, 0))
    return main, any3, half3, start3


def kernel(p_hbm, ap_hbm, pp_ref, app_ref, out_ref, pbuf, apbuf, load_sem,
           psend, prelay, precv, apsend, aprelay, aprecv, aprelayed):
    r = lax.axis_index("row")
    c = lax.axis_index("col")
    z = c % 4
    core = r % 2
    y2 = r - core
    own_main, own_any, own_half, own_start = shape_of(r, c)
    step = jnp.where(z < 2, -2, 2)
    relay_slot = jnp.where(z < 2, 0, 4)
    relay_source = (c + jnp.where(z < 2, -2, 2) + COLS) % COLS
    relay_main, relay_any, relay_half, relay_start = shape_of(r, relay_source)

    def ap_slot(row, half):
        v = 2 * row + half - c
        far = (v == 8) | (v == -8)
        near = (v >= -2) & (v <= 2)
        return near | far, jnp.where(far, FAR, jnp.where(near, v + 2, 0))

    p_targets = [
        (own_any, (c + step + COLS) % COLS, 2 - step),
        (own_any & (z != 3), (c + 1) % COLS, 1),
        (own_any & (z != 0), (c + COLS - 1) % COLS, 3),
    ]
    back = jnp.where(z < 2, -2, 2)
    p_relays = [
        (relay_any, (relay_source + back + COLS) % COLS, 2 - back),
        (relay_any, (relay_source + 8) % COLS, FAR),
        (
            relay_any & (((z == 1) & (relay_source < COLS - 1)) | ((z == 2) & (relay_source > 0))),
            jnp.where(z == 1, relay_source + 1, relay_source - 1 + COLS) % COLS,
            jnp.where(z == 1, 1, 3),
        ),
    ]
    ap_own = []
    for half in range(2):
        wanted, there = ap_slot(r, half)
        if half == 0:
            onward = jnp.where(core == 0, (r + 7) % ROWS, (r + 6) % ROWS)
            to_buffer = jnp.where(core == 0, 2 + there, RELAYED)
            across = wanted & (core == 1)
        else:
            onward = jnp.where(core == 1, (r + 1) % ROWS, (r + 2) % ROWS)
            to_buffer = jnp.where(core == 1, 2 + there, RELAYED)
            across = wanted & (core == 0)
        other = y2 + 1 - core
        ap_own.append((half, wanted, there, onward, to_buffer, across, other))
    facing = jnp.where(core == 1, (r + 1) % ROWS, (r + 7) % ROWS)
    alike = jnp.where(core == 1, (r + 2) % ROWS, (r + 6) % ROWS)
    half_in = 1 - core
    facing_wanted, facing_slot = ap_slot(facing, half_in)
    alike_wanted, alike_slot = ap_slot(alike, half_in)

    def narrow(slot):
        return (slot == 0) | (slot == 4) | (slot == FAR)

    def p_copy(piece, source_slot, target, slot, half, start, send):
        at, size = ((0, 2), (2, 2), (start, 2), (start + 2, 1))[piece]
        return pltpu.make_async_remote_copy(
            src_ref=pbuf.at[source_slot, half, pl.ds(at, size)],
            dst_ref=pbuf.at[slot, half, pl.ds(at, size)],
            send_sem=send,
            recv_sem=precv.at[slot, piece],
            device_id=(r, target),
            device_id_type=MESH,
        )

    def each_ap_piece(slot, act):
        act(0, jnp.where(slot == 4, 1, 0), 2)

        @pl.when(narrow(slot))
        def _():
            act(1, jnp.where(slot == 4, 3, 2), 1)

        @pl.when(jnp.logical_not(narrow(slot)))
        def _():
            act(1, 2, 2)

    def ap_copy(at, size, source, target, buffer, send, recv):
        return pltpu.make_async_remote_copy(
            src_ref=apbuf.at[source, pl.ds(at, size)],
            dst_ref=apbuf.at[buffer, pl.ds(at, size)],
            send_sem=send,
            recv_sem=recv,
            device_id=(target, c),
            device_id_type=MESH,
        )

    barrier = pltpu.get_barrier_semaphore()

    def greet(present, row, col):
        @pl.when(present)
        def _():
            pl.semaphore_signal(barrier, inc=1, device_id=(row, col), device_id_type=MESH)

    for slot in (1, 3):
        cp, ok = column_of(c, slot)
        present = ok & shape_of(r, cp)[1]
        via = (cp % 4) == (3 if slot == 1 else 0)
        sender = jnp.where(via, (cp + (2 if slot == 1 else COLS - 2)) % COLS, (cp + COLS) % COLS)
        greet(present, r, sender)
    greet(relay_any, r, relay_source)
    ring = jnp.where(z < 2, c + 2, c - 2)
    greet(shape_of(r, ring)[1], r, (c + jnp.where(z < 2, 4, 12)) % COLS)
    across_c = (c + 8) % COLS
    greet(shape_of(r, across_c)[1], r, (across_c + step + COLS) % COLS)
    greet(facing_wanted, facing, c)
    greet(alike_wanted, alike, c)
    other = y2 + 1 - core
    greet(ap_slot(other, core)[0], other, c)
    far_row = (r + 4) % ROWS
    for half in range(2):
        if half == 0:
            sender = jnp.where(core == 0, (far_row + 7) % ROWS, (far_row + 6) % ROWS)
        else:
            sender = jnp.where(core == 1, (far_row + 1) % ROWS, (far_row + 2) % ROWS)
        greet(ap_slot(far_row, half)[0], sender, c)

    expected = jnp.int32(0)
    p_exists = [own_any, own_any & (z != 3), own_any & (z != 0)]
    for present in [
        *p_exists,
        *[present for present, _, _ in p_relays],
        *[wanted for _, wanted, _, _, _, _, _ in ap_own],
        *[across for _, _, _, _, _, across, _ in ap_own],
        facing_wanted,
        alike_wanted,
    ]:
        expected = expected + jnp.where(present, 1, 0)

    loads = []
    for g in range(2):
        for i in range(4):
            loads.append(pltpu.make_async_copy(
                p_hbm.at[pl.ds(g * GROUP, GROUP), pl.ds(i * TILE, TILE)],
                pbuf.at[OWN, i // 2, 2 * g + 1 - i % 2],
                load_sem.at[4 * g + i],
            ))
    for q in range(4):
        for j in range(2):
            loads.append(pltpu.make_async_copy(
                ap_hbm.at[pl.ds(q * GROUP, GROUP), pl.ds(j * TILE, TILE)],
                apbuf.at[q // 2, 2 * j + 1 - q % 2],
                load_sem.at[8 + 2 * q + j],
            ))
    for load in loads:
        load.start()
    out_ref[...] = jnp.zeros_like(out_ref)
    blank = jnp.zeros((GROUP, TILE), jnp.bfloat16)
    apbuf[2 + 0, 3] = blank
    apbuf[2 + 4, 0] = blank
    apbuf[2 + FAR, 3] = blank
    for slot in range(SLOTS):
        if slot != OWN:
            cp, ok = column_of(c, slot)
            _, any3, half, start = shape_of(r, cp)

            @pl.when(ok & any3)
            def _():
                pbuf[slot, half, jnp.where(start == 0, 3, 0)] = blank
    for load in loads:
        load.wait()
    for a in range(6):
        g, rows = a // 3, pl.ds(a % 3 * TILE, TILE)
        for i in range(4):
            weight = pp_ref[i, a].astype(jnp.float32).astype(jnp.bfloat16)
            slab = (OWN, i // 2, 2 * g + 1 - i % 2, rows)
            pbuf[slab] = pbuf[slab] * weight
    for a in range(12):
        q, rows = a // 3, pl.ds(a % 3 * TILE, TILE)
        for j in range(2):
            weight = app_ref[j, a].astype(jnp.float32).astype(jnp.bfloat16)
            slab = (q // 2, 2 * j + 1 - q % 2, rows)
            apbuf[slab] = apbuf[slab] * weight

    @pl.when(expected > 0)
    def _():
        pl.semaphore_wait(barrier, expected)

    def each_own_p(piece, act):
        @pl.when(own_main if piece < 2 else own_any)
        def _():
            half = c % 2 if piece < 2 else own_half
            for n, (present, target, slot) in enumerate(p_targets):
                @pl.when(present)
                def _():
                    act(p_copy(piece, OWN, target, slot, half, own_start, psend.at[n, piece]))

    def each_relay_p(piece, act, arrive=None):
        @pl.when(relay_main if piece < 2 else relay_any)
        def _():
            half = relay_source % 2 if piece < 2 else relay_half
            if arrive is not None:
                p_copy(piece, OWN, c, relay_slot, half, relay_start, prelay.at[0, piece]).wait_recv()
            for n, (present, target, slot) in enumerate(p_relays):
                @pl.when(present)
                def _():
                    act(p_copy(piece, relay_slot, target, slot, half, relay_start, prelay.at[n, piece]))

    def each_own_ap(act):
        for half, wanted, there, onward, to_buffer, across, other in ap_own:
            @pl.when(wanted)
            def _():
                def one(piece, at, size):
                    kept = to_buffer != RELAYED

                    @pl.when(kept)
                    def _():
                        act(ap_copy(at, size, half, onward, to_buffer, apsend.at[half, 0, piece], aprecv.at[there, piece]))

                    @pl.when(jnp.logical_not(kept))
                    def _():
                        act(ap_copy(at, size, half, onward, RELAYED, apsend.at[half, 0, piece], aprelayed.at[piece]))

                    @pl.when(across)
                    def _():
                        act(ap_copy(at, size, half, other, 2 + there, apsend.at[half, 1, piece], aprecv.at[there, piece]))

                each_ap_piece(there, one)

    def each_relay_ap(act, arrive):
        for n, (wanted, source, slot, buffer) in enumerate((
            (alike_wanted, alike, alike_slot, RELAYED),
            (facing_wanted, facing, facing_slot, 2 + facing_slot),
        )):
            @pl.when(wanted)
            def _():
                def one(piece, at, size):
                    recv = aprelayed.at[piece] if n == 0 else aprecv.at[slot, piece]
                    if arrive:
                        ap_copy(at, size, 0, r, buffer, aprelay.at[n, piece], recv).wait_recv()
                    act(ap_copy(
                        at, size, buffer, (source + 4) % ROWS, 2 + slot,
                        aprelay.at[n, piece], aprecv.at[slot, piece],
                    ))

                each_ap_piece(slot, one)

    def start(copy):
        copy.start()

    def wait_send(copy):
        copy.wait_send()

    for piece in (2, 0, 1, 3):
        each_own_p(piece, start)
        if piece == 2:
            each_own_ap(start)
    each_relay_p(2, start, True)
    each_relay_p(0, start, True)
    each_relay_ap(start, True)
    each_relay_p(1, start, True)
    each_relay_p(3, start, True)

    def multiply(n, carry):
        order = n // 2
        t = n % 2
        slot = jnp.where(order == 0, OWN, jnp.where(order == 1, 1, jnp.where(
            order == 2, 3, jnp.where(order == 3, relay_slot, jnp.where(order == 4, 4 - relay_slot, FAR)))))
        cp, ok = column_of(c, slot)
        main, any3, half3, start3 = shape_of(r, cp)
        m, h = cp // 2, cp % 2
        full = ok & main & (t == h)
        part = ok & any3 & (t == half3)
        waits = (slot != OWN) & (slot != relay_slot)

        @pl.when(t == 0)
        def _():
            remote = ok & any3 & (m != r)
            faced = ((core == 1) & (m == r + 1)) | ((core == 0) & (m == r - 1))

            @pl.when(remote & jnp.logical_not(faced))
            def _():
                def one(piece, at, size):
                    ap_copy(at, size, 0, r, 2 + slot, aprelay.at[0, piece], aprecv.at[slot, piece]).wait_recv()

                each_ap_piece(slot, one)

        @pl.when(full & waits)
        def _():
            for piece in (0, 1):
                p_copy(piece, OWN, c, slot, t, 0, psend.at[0, piece]).wait_recv()

        @pl.when(part & waits)
        def _():
            for piece in (2, 3):
                p_copy(piece, OWN, c, slot, t, start3, psend.at[0, piece]).wait_recv()

        @pl.when(full | part)
        def _():
            ap_index = jnp.where(m == r, h, 2 + slot)
            rows = pl.ds(pl.multiple_of(t * HALF, HALF), HALF)
            left = jnp.concatenate([
                jnp.concatenate([pbuf[slot, t, 2 * g + 1], pbuf[slot, t, 2 * g]], axis=1) for g in range(2)
            ], axis=0)
            right = jnp.concatenate([
                jnp.concatenate([apbuf[ap_index, 1 - g], apbuf[ap_index, 3 - g]], axis=1) for g in range(2)
            ], axis=0)
            out_ref[rows, :] += lax.dot_general(
                left, right, (((0,), (0,)), ((), ())), preferred_element_type=jnp.float32
            )

        return carry

    lax.fori_loop(0, 2 * SLOTS, multiply, 0)

    for piece in range(4):
        each_own_p(piece, wait_send)
    each_own_ap(wait_send)
    for piece in range(4):
        each_relay_p(piece, wait_send)
    each_relay_ap(wait_send, False)


def on_device(prolong, applied, prolong_pattern, applied_pattern):
    return pl.pallas_call(
        kernel,
        out_shape=jax.ShapeDtypeStruct((prolong.shape[1], applied.shape[1]), jnp.float32),
        in_specs=[
            pl.BlockSpec(memory_space=pl.ANY),
            pl.BlockSpec(memory_space=pl.ANY),
            pl.BlockSpec(memory_space=pltpu.SMEM),
            pl.BlockSpec(memory_space=pltpu.SMEM),
        ],
        out_specs=pl.BlockSpec(memory_space=pltpu.VMEM),
        scratch_shapes=[
            pltpu.VMEM((SLOTS, 2, 4, GROUP, TILE), jnp.bfloat16),
            pltpu.VMEM((3 + SLOTS, 4, GROUP, TILE), jnp.bfloat16),
            pltpu.SemaphoreType.DMA((16,)),
            pltpu.SemaphoreType.DMA((3, 4)),
            pltpu.SemaphoreType.DMA((3, 4)),
            pltpu.SemaphoreType.DMA((SLOTS, 4)),
            pltpu.SemaphoreType.DMA((2, 2, 2)),
            pltpu.SemaphoreType.DMA((2, 2)),
            pltpu.SemaphoreType.DMA((SLOTS, 2)),
            pltpu.SemaphoreType.DMA((2,)),
        ],
        compiler_params=pltpu.CompilerParams(
            collective_id=0, has_side_effects=True, vmem_limit_bytes=63 * 1024 * 1024
        ),
    )(prolong, applied, prolong_pattern.T, applied_pattern.T)


def solution(mesh):
    in_specs = (P("col", "row"), P("row", "col"), P("col", "row"), P("row", "col"))
    out_specs = P("row", "col")
    return jax.shard_map(
        on_device, mesh=mesh, in_specs=in_specs, out_specs=out_specs, check_vma=False
    )
```

```python
import collections

import jax
import jax.numpy as jnp
from jax import lax
from jax.experimental import pallas as pl
from jax.experimental.pallas import tpu as pltpu
from jax.sharding import PartitionSpec as P

MESH = pl.DeviceIdType.MESH
TILE = 128
ROWS = 8
COLS = 16
GROUP = 384
HALF = 256
FAR = 5
OWN = 2
SLOTS = 6
ORDER = (OWN, 1, 3, 0, 4, FAR)
SOURCE = -1
RELAY = 5
ACROSS = 6
EVERY = frozenset(range(4))

ROUTES = (
    (-1, -1, -1, 0, 1, 0, -1, 262, 87, 471, 142, 377, 426, 68, 75, 155, 235, 156, 0),
    (33, 5, -1, 1, 5, 5, -1, 436, 393, 275, 102, 16, 75, 234, 125, 238, 149, 196, 64),
    (48, 5, -1, 1, 5, -1, -1, 238, 84, 458, 18, 475, 416, 181, 30, 152, 213, 116, 48),
    (19, 2, 2, -1, 5, 5, -1, 53, 34, 282, 83, 104, 29, 222, 150, 98, 194, 176, 15),
    (48, 5, -1, 4, 5, -1, -1, 171, 210, 301, 468, 427, 225, 172, 120, 241, 242, 124, 137),
    (48, 5, -1, 5, 5, 5, -1, 312, 235, 376, 152, 150, 95, 124, 174, 236, 218, 232, 84),
    (33, -1, -1, 5, 5, 1, -1, 91, 123, 76, 404, 429, 4, 40, 73, 230, 220, 226, 114),
    (51, 5, -1, 5, 5, 5, -1, 111, 112, 82, 26, 138, 353, 148, 29, 186, 170, 190, 49),
    (-1, -1, -1, 0, 4, -1, -1, 5, 324, 387, 229, 59, 89, 62, 147, 208, 229, 111, 0),
    (-1, -1, -1, 1, 0, 0, -1, 425, 174, 323, 85, 188, 469, 90, 101, 204, 221, 233, 0),
    (-1, -1, 3, 0, -1, -1, -1, 433, 420, 465, 2, 116, 168, 81, 109, 171, 19, 21, 0),
    (-1, -1, -1, 0, 0, 0, -1, 357, 396, 359, 128, 462, 100, 38, 36, 94, 128, 103, 0),
    (-1, -1, -1, -1, -1, -1, -1, 232, 445, 54, 246, 241, 99, 43, 88, 192, 100, 92, 0),
    (-1, -1, -1, 0, 1, -1, -1, 428, 107, 317, 463, 60, 403, 112, 47, 219, 131, 52, 0),
    (-1, -1, -1, 4, 1, -1, -1, 293, 332, 172, 214, 43, 272, 4, 9, 138, 198, 7, 0),
    (51, 5, -1, 5, 5, 5, -1, 365, 12, 473, 161, 72, 424, 103, 1, 159, 113, 121, 18),
    (33, 5, 5, 5, 5, 5, -1, 280, 37, 192, 44, 41, 58, 225, 134, 169, 67, 187, 31),
    (3, 2, 5, -1, 2, 5, -1, 167, 392, 207, 263, 64, 447, 175, 237, 25, 122, 173, 65),
    (-1, -1, -1, 1, 4, -1, -1, 330, 338, 297, 62, 432, 244, 16, 78, 178, 177, 56, 0),
    (51, 5, -1, 5, 5, 5, -1, 202, 296, 271, 276, 366, 184, 72, 37, 162, 110, 132, 8),
    (-1, -1, -1, 0, 1, -1, -1, 134, 105, 316, 321, 419, 40, 34, 74, 153, 168, 130, 0),
    (44, -1, 5, 5, 5, -1, -1, 406, 24, 240, 322, 431, 73, 144, 182, 142, 217, 180, 55),
    (-1, -1, -1, 0, 1, 1, -1, 343, 204, 15, 298, 252, 421, 96, 123, 210, 216, 207, 0),
    (-1, 4, 2, -1, 4, -1, -1, 206, 285, 278, 444, 213, 286, 197, 214, 90, 189, 70, 0),
    (48, 5, 3, 3, -1, -1, -1, 239, 120, 369, 434, 448, 211, 166, 189, 193, 85, 71, 64),
    (-1, -1, 3, 3, -1, 0, -1, 212, 70, 101, 177, 461, 137, 24, 91, 91, 26, 154, 0),
    (-1, -1, -1, -1, 2, -1, -1, 329, 408, 19, 135, 360, 233, 35, 54, 22, 105, 57, 0),
    (-1, -1, 0, 0, -1, -1, -1, 261, 456, 197, 131, 69, 209, 5, 185, 141, 28, 8, 0),
    (-1, -1, -1, 0, 0, -1, -1, 442, 268, 300, 334, 50, 385, 53, 89, 161, 160, 42, 0),
    (-1, 2, -1, -1, 2, -1, -1, 32, 349, 21, 140, 256, 33, 209, 117, 59, 140, 69, 0),
    (-1, 2, -1, -1, 2, -1, -1, 290, 306, 260, 71, 451, 164, 200, 126, 79, 183, 135, 0),
    (-1, -1, -1, -1, 2, -1, -1, 201, 289, 314, 86, 265, 156, 23, 76, 102, 202, 61, 0),
    (-1, -1, -1, -1, -1, -1, -1, 479, 234, 11, 122, 93, 28, 165, 83, 0, 0, 0, 0),
    (-1, 1, -1, -1, -1, -1, -1, 460, 49, 305, 351, 470, 395, 139, 39, 0, 0, 0, 0),
    (-1, -1, -1, -1, -1, -1, -1, 81, 414, 242, 25, 79, 437, 0, 184, 0, 0, 0, 0),
    (-1, -1, -1, -1, -1, -1, -1, 249, 361, 386, 114, 370, 327, 0, 136, 0, 0, 0, 0),
    (12, 5, 5, -1, -1, -1, -1, 162, 443, 337, 455, 132, 388, 95, 143, 0, 0, 0, 60),
    (12, 5, 5, -1, -1, -1, -1, 292, 126, 302, 378, 139, 407, 146, 195, 0, 0, 0, 104),
    (4, -1, 5, -1, -1, -1, -1, 320, 185, 175, 450, 401, 17, 0, 212, 0, 0, 0, 112),
    (9, 5, 5, -1, -1, -1, -1, 453, 57, 328, 153, 151, 364, 0, 205, 0, 0, 0, 106),
    (-1, -1, -1, -1, -1, -1, -1, 368, 148, 288, 309, 199, 415, 227, 211, 0, 0, 0, 0),
    (15, 5, 5, -1, -1, -1, -1, 158, 250, 269, 144, 97, 411, 201, 223, 0, 0, 0, 119),
    (-1, -1, -1, -1, -1, -1, -1, 389, 325, 159, 166, 236, 46, 0, 239, 0, 0, 0, 0),
    (9, -1, 5, -1, -1, -1, -1, 190, 299, 154, 438, 394, 430, 0, 231, 0, 0, 0, 127),
    (-1, 1, -1, -1, -1, -1, -1, 391, 27, 224, 410, 3, 119, 0, 206, 0, 0, 0, 0),
    (-1, 1, -1, -1, -1, -1, -1, 228, 476, 121, 284, 397, 270, 0, 228, 0, 0, 0, 0),
    (-1, -1, 0, -1, -1, -1, -1, 181, 52, 307, 208, 133, 226, 13, 82, 0, 0, 0, 0),
    (-1, -1, -1, -1, -1, -1, -1, 259, 277, 283, 39, 454, 47, 32, 44, 0, 0, 0, 0),
    (-1, -1, -1, -1, -1, -1, -1, 169, 237, 98, 319, 222, 295, 0, 77, 0, 0, 0, 0),
    (-1, -1, -1, -1, -1, -1, -1, 382, 231, 374, 348, 310, 36, 0, 33, 0, 0, 0, 0),
    (28, 5, -1, -1, -1, -1, -1, 68, 35, 31, 344, 0, 124, 0, 2, 0, 0, 0, 0),
    (-1, -1, 0, -1, -1, -1, -1, 362, 245, 398, 186, 273, 464, 0, 3, 0, 0, 0, 0),
    (4, -1, 5, -1, -1, -1, -1, 90, 20, 477, 77, 218, 103, 0, 139, 0, 0, 0, 20),
    (16, 5, -1, -1, -1, -1, -1, 165, 6, 342, 372, 146, 198, 0, 11, 0, 0, 0, 0),
    (-1, 1, -1, -1, -1, -1, -1, 457, 251, 42, 170, 178, 423, 163, 63, 0, 0, 0, 0),
    (7, 5, 5, -1, -1, -1, -1, 345, 106, 346, 109, 422, 96, 93, 133, 0, 0, 0, 17),
    (-1, 1, -1, -1, -1, -1, -1, 155, 418, 449, 66, 474, 375, 0, 164, 0, 0, 0, 0),
    (-1, -1, -1, -1, -1, -1, -1, 440, 193, 347, 194, 147, 459, 0, 66, 0, 0, 0, 0),
    (-1, 1, -1, -1, -1, -1, -1, 318, 409, 230, 472, 143, 373, 199, 111, 0, 0, 0, 0),
    (-1, 1, -1, -1, -1, -1, -1, 65, 180, 117, 149, 173, 215, 115, 22, 0, 0, 0, 0),
    (-1, -1, 0, -1, -1, -1, -1, 141, 266, 74, 326, 129, 113, 0, 224, 0, 0, 0, 0),
    (14, 5, -1, -1, -1, -1, -1, 379, 78, 136, 412, 80, 22, 0, 80, 0, 0, 0, 0),
    (-1, 1, -1, -1, -1, -1, -1, 467, 217, 145, 294, 311, 55, 240, 179, 0, 0, 0, 0),
    (-1, 1, -1, -1, -1, -1, -1, 257, 88, 281, 254, 335, 304, 215, 129, 0, 0, 0, 0),
    (-1, 1, -1, -1, -1, -1, -1, 176, 383, 358, 223, 196, 10, 0, 145, 0, 0, 0, 0),
    (-1, -1, 0, -1, -1, -1, -1, 380, 67, 287, 452, 313, 243, 0, 14, 0, 0, 0, 0),
    (-1, 1, -1, -1, -1, -1, -1, 92, 279, 341, 163, 402, 1, 191, 99, 0, 0, 0, 0),
    (-1, -1, -1, -1, -1, -1, -1, 446, 182, 439, 331, 110, 56, 151, 58, 0, 0, 0, 0),
    (-1, 1, -1, -1, -1, -1, -1, 7, 30, 38, 195, 13, 23, 118, 12, 0, 0, 0, 0),
    (-1, -1, 0, -1, -1, -1, -1, 130, 253, 51, 94, 315, 48, 6, 158, 0, 0, 0, 0),
    (-1, -1, 0, -1, -1, -1, -1, 108, 339, 127, 220, 367, 478, 0, 27, 0, 0, 0, 0),
    (-1, -1, 0, -1, -1, -1, -1, 203, 352, 200, 216, 179, 400, 0, 51, 0, 0, 0, 0),
    (-1, -1, -1, -1, -1, -1, -1, 336, 125, 157, 441, 248, 219, 86, 45, 0, 0, 0, 0),
    (-1, -1, -1, -1, -1, -1, -1, 303, 435, 160, 264, 363, 354, 41, 97, 0, 0, 0, 0),
    (-1, 1, -1, -1, -1, -1, -1, 371, 405, 115, 267, 333, 247, 167, 50, 0, 0, 0, 0),
    (-1, 1, -1, -1, -1, -1, -1, 61, 390, 350, 355, 291, 356, 107, 10, 0, 0, 0, 0),
    (-1, 1, -1, -1, -1, -1, -1, 45, 14, 413, 63, 191, 466, 188, 87, 0, 0, 0, 0),
    (-1, -1, -1, -1, -1, -1, -1, 227, 340, 187, 118, 221, 189, 108, 157, 0, 0, 0, 0),
    (-1, 1, -1, -1, -1, -1, -1, 399, 381, 205, 384, 183, 9, 0, 203, 0, 0, 0, 0),
    (-1, -1, -1, -1, -1, -1, -1, 417, 8, 255, 258, 308, 274, 0, 46, 0, 0, 0, 0),
)


def chip_of(device):
    return device[1] // 4, device[0] // 2, device[1] % 4


def role_of(device):
    x, y, z = chip_of(device)
    return (x - y) % 4, z, device[0] % 2


def p_kind(r, cp):
    m, h = cp // 2, cp % 2
    if m == r:
        return 0
    if (m == r + 1 and h == 0) or (m == r - 1 and h == 1):
        return 1
    return 2 if m == (r + 4) % ROWS else None


def p_pieces(kind, h):
    if kind == 0:
        return ((h, 0, 2, 0), (h, 2, 2, 1), (1 - h, 1 - h, 2, 2), (1 - h, 3 - h, 1, 3))
    half, start = (1 - h, h) if kind == 1 else (h, 0)
    return ((half, start, 2, 2), (half, start + 2, 1, 3))


def ap_pieces(slot):
    if slot == 4:
        return ((1, 2, 0), (3, 1, 1))
    return ((0, 2, 0), (2, 1 if slot in (0, FAR) else 2, 1))


def pieces():
    found = collections.OrderedDict()
    for r in range(ROWS):
        for cp in range(COLS):
            kind = p_kind(r, cp)
            if kind is None:
                continue
            z = cp % 4
            for n, (half, at, size, piece) in enumerate(p_pieces(kind, z % 2)):
                users = {n: (r, cp + d) for n, d in enumerate((-1, 1, -2, 2)) if 0 <= cp + d < COLS}
                users[4] = (r, (cp + 8) % COLS)
                entry = found.setdefault((0, kind, z, n), ((half, at, size, piece), []))
                entry[1].append(((r, cp), users))
    for r in range(ROWS):
        for c in range(COLS):
            for half in range(2):
                v = 2 * r + half - c
                slot = v + 2 if -2 <= v <= 2 else FAR if v in (8, -8) else None
                if slot is None:
                    continue
                x, y, z = chip_of((r, c))
                side = r - 1 + 2 * half
                for n, (at, size, piece) in enumerate(ap_pieces(slot)):
                    users = {1: ((r + 4) % ROWS, c)}
                    if 0 <= side < ROWS:
                        users[0 if side // 2 != r // 2 else ACROSS] = (side, c)
                    key = (1, r % 2, half, (x - y) % 4, z, n)
                    entry = found.setdefault(key, ((slot, half, at, size, piece), []))
                    entry[1].append(((r, c), users))
    return found


P_SLOT = (3, 1, 4, 0, FAR)

class Role:
    def __init__(self):
        self.sends = {}
        self.arrivals = {}
        self.greets = {}
        self.partners = {y: set() for y in range(4)}
        self.relayed = {}
        self.slabs = 0


def move_between(a, b):
    (ax, ay, _), (bx, by, bz) = chip_of(a), chip_of(b)
    return (bx - ax) % 4, (by - ay) % 4, bz, b[0] % 2


def make_plan():
    roles = {(a, z, core): Role() for a in range(4) for z in range(4) for core in range(2)}
    kinds = list(pieces().items())
    for n, (key, (_, instances)) in enumerate(kinds):
        size = kinds[n][1][0][3] if key[0] else kinds[n][1][0][2]
        offset, parents = ROUTES[n][0], ROUTES[n][1:7]
        for source, users in instances:
            place = dict(users)
            x, y, z = chip_of(source)
            if offset >= 0:
                rx, ry, rz = (x + offset % 4) % 4, (y + offset // 4 % 4) % 4, (z + offset // 16) % 4
                place[RELAY] = (2 * ry + source[0] % 2, 4 * rx + rz)
            place[SOURCE] = source
            reached = {SOURCE: SOURCE}
            edges = []

            def reach(node):
                if node in reached:
                    return reached[node]
                up = SOURCE if node == ACROSS else parents[node]
                if node not in place:
                    reached[node] = reach(up)
                    return reached[node]
                same = [u for u in users if node == RELAY and users[u] == place[RELAY]]
                if node == RELAY and place[RELAY] == source:
                    reached[node] = SOURCE
                    return SOURCE
                if same:
                    reached[same[0]] = same[0]
                    reached[node] = same[0]
                    edges.append((reach(up), same[0]))
                    return same[0]
                reached[node] = node
                edges.append((reach(up), node))
                return node

            if RELAY in place and RELAY in [parents[u] for u in users if u != ACROSS]:
                reach(RELAY)
            for user in users:
                reach(user)
            for a, b in edges:
                here, there = place[a], place[b]
                assert here != there
                mine, theirs = roles[role_of(here)], roles[role_of(there)]
                edge = (n, a, b, move_between(here, there))
                mine.sends.setdefault(edge, set()).add(here[0] // 2)
                theirs.arrivals.setdefault((n, b), set()).add(there[0] // 2)
                theirs.greets.setdefault(move_between(there, here), set()).add(there[0] // 2)
                mine.partners[here[0] // 2].add(there)
                if b == RELAY and n not in theirs.relayed:
                    theirs.relayed[n] = (theirs.slabs, len(theirs.relayed))
                    theirs.slabs += size
    return kinds, roles


KINDS, PLAN = make_plan()
MOST_SENDS = max(len(role.sends) for role in PLAN.values())
MOST_SLABS = max(max(role.slabs for role in PLAN.values()), 1)
MOST_RELAYED = max(max(len(role.relayed) for role in PLAN.values()), 1)


def target_role(role, move):
    return (role[0] + move[0] - move[1]) % 4, move[2], move[3]


def column_of(c, slot):
    near = c + slot - 2
    far = slot == FAR
    cp = jnp.where(far, (c + 8) % COLS, near)
    return cp, far | ((near >= 0) & (near < COLS))


def shape_of(r, cp):
    m, h = cp // 2, cp % 2
    main = m == r
    low = (m == r + 1) & (h == 0)
    high = (m == r - 1) & (h == 1)
    far = m == (r + 4) % ROWS
    any3 = main | low | high | far
    half3 = jnp.where(far, h, 1 - h)
    start3 = jnp.where(main, 1 - h, jnp.where(high, 1, 0))
    return main, any3, half3, start3


def kernel(p_hbm, ap_hbm, pp_ref, app_ref, out_ref, pbuf, apbuf, relaybuf, load_sem, send_sem, precv, aprecv, relayrecv):
    r = lax.axis_index("row")
    c = lax.axis_index("col")
    x, y, z, core = c // 4, r // 2, c % 4, r % 2
    diagonal = (x - y + 4) % 4
    is_y = [y == n for n in range(4)]

    def for_members(members, act):
        if members == EVERY:
            act()
        elif members:
            test = None
            for n in sorted(members):
                test = is_y[n] if test is None else test | is_y[n]
            pl.when(test)(act)

    def for_roles(act):
        def for_z(a):
            for zz in range(4):
                def for_core(zz=zz):
                    for cc in range(2):
                        pl.when(core == cc)(lambda cc=cc: act((a, zz, cc)))
                pl.when(z == zz)(for_core)
        for a in range(4):
            pl.when(diagonal == a)(lambda a=a: for_z(a))

    def device(move):
        return 2 * ((y + move[1]) % 4) + move[3], 4 * ((x + move[0]) % 4) + move[2]

    def region(n, node, role):
        key, (shape, _) = KINDS[n]
        if node == RELAY:
            first, index = PLAN[role].relayed[n]
            size = shape[3] if key[0] else shape[2]
            return relaybuf.at[pl.ds(first, size)], relayrecv.at[index]
        if key[0] == 0:
            half, at, size, piece = shape
            slot = OWN if node == SOURCE else P_SLOT[node]
            return pbuf.at[slot, half, pl.ds(at, size)], precv.at[slot, piece]
        slot, half, at, size, piece = shape
        return apbuf.at[half if node == SOURCE else 2 + slot, pl.ds(at, size)], aprecv.at[slot, piece]

    def copy_of(role, edge):
        n, a, b, move = edge
        source, _ = region(n, a, role)
        target, recv = region(n, b, target_role(role, move))
        return pltpu.make_async_remote_copy(
            src_ref=source,
            dst_ref=target,
            send_sem=send_sem.at[list(PLAN[role].sends).index(edge)],
            recv_sem=recv,
            device_id=device(move),
            device_id_type=MESH,
        )

    def arrived(role, n, node):
        target, recv = region(n, node, role)
        pltpu.make_async_remote_copy(
            src_ref=target, dst_ref=target, send_sem=send_sem.at[0], recv_sem=recv,
            device_id=(r, c), device_id_type=MESH,
        ).wait_recv()

    def order_of(edge):
        n, _, b, _ = edge
        return -1 if b == ACROSS else ROUTES[n][7 + b]

    def passed_on(role):
        found = {}
        for (n, a, _, _), members in PLAN[role].sends.items():
            if a != SOURCE:
                found.setdefault((n, a), set()).update(members)
        return found

    barrier = pltpu.get_barrier_semaphore()

    def greet(role):
        for move, members in sorted(PLAN[role].greets.items()):
            for_members(members, lambda move=move: pl.semaphore_signal(
                barrier, inc=1, device_id=device(move), device_id_type=MESH))

    def send(role):
        plan = PLAN[role]
        counts = {}
        for n, partners in plan.partners.items():
            counts.setdefault(len(partners), set()).add(n)
        for count, members in counts.items():
            if count:
                for_members(members, lambda count=count: pl.semaphore_wait(barrier, count))
        for edge in sorted((e for e in plan.sends if e[1] == SOURCE), key=order_of):
            for_members(plan.sends[edge], lambda edge=edge: copy_of(role, edge).start())
        waits = sorted(passed_on(role).items(), key=lambda item: ROUTES[item[0][0]][13 + item[0][1]])
        for (n, node), members in waits:
            for_members(members, lambda n=n, node=node: arrived(role, n, node))
            for edge in sorted((e for e in plan.sends if e[:2] == (n, node)), key=order_of):
                for_members(plan.sends[edge], lambda edge=edge: copy_of(role, edge).start())

    def finish(role):
        for edge, members in PLAN[role].sends.items():
            for_members(members, lambda edge=edge: copy_of(role, edge).wait_send())

    def await_step(step):
        def one(role):
            handed = passed_on(role)
            by_step = {}
            for (n, node), members in PLAN[role].arrivals.items():
                left = members - handed.get((n, node), set())
                if node == RELAY or not left:
                    continue
                key, (shape, _) = KINDS[n]
                at = 2 * ORDER.index(shape[0]) if key[0] else 2 * ORDER.index(P_SLOT[node]) + shape[0]
                by_step.setdefault(at, []).append((n, node, left))
            for at, waits in sorted(by_step.items()):
                @pl.when(step == at)
                def _():
                    for n, node, left in waits:
                        for_members(left, lambda n=n, node=node: arrived(role, n, node))

        for_roles(one)

    for_roles(greet)

    loads = []
    for g in range(2):
        for i in range(4):
            loads.append(pltpu.make_async_copy(
                p_hbm.at[pl.ds(g * GROUP, GROUP), pl.ds(i * TILE, TILE)],
                pbuf.at[OWN, i // 2, 2 * g + 1 - i % 2],
                load_sem.at[4 * g + i],
            ))
    for q in range(4):
        for j in range(2):
            loads.append(pltpu.make_async_copy(
                ap_hbm.at[pl.ds(q * GROUP, GROUP), pl.ds(j * TILE, TILE)],
                apbuf.at[q // 2, 2 * j + 1 - q % 2],
                load_sem.at[8 + 2 * q + j],
            ))
    for load in loads:
        load.start()
    for load in loads:
        load.wait()
    for a in range(6):
        g, rows = a // 3, pl.ds(a % 3 * TILE, TILE)
        for i in range(4):
            weight = pp_ref[i, a].astype(jnp.float32).astype(jnp.bfloat16)
            slab = (OWN, i // 2, 2 * g + 1 - i % 2, rows)
            pbuf[slab] = pbuf[slab] * weight
    for a in range(12):
        q, rows = a // 3, pl.ds(a % 3 * TILE, TILE)
        for j in range(2):
            weight = app_ref[j, a].astype(jnp.float32).astype(jnp.bfloat16)
            slab = (q // 2, 2 * j + 1 - q % 2, rows)
            apbuf[slab] = apbuf[slab] * weight

    for_roles(send)

    blank = jnp.zeros((GROUP, TILE), jnp.bfloat16)
    apbuf[2 + 0, 3] = blank
    apbuf[2 + 4, 0] = blank
    apbuf[2 + FAR, 3] = blank
    for slot in range(SLOTS):
        if slot != OWN:
            cp, ok = column_of(c, slot)
            _, any3, half, start = shape_of(r, cp)

            @pl.when(ok & any3)
            def _():
                pbuf[slot, half, jnp.where(start == 0, 3, 0)] = blank
    out_ref[...] = jnp.zeros_like(out_ref)

    def multiply(step, carry):
        t = step % 2
        slot = jnp.int32(ORDER[0])
        for n in range(1, SLOTS):
            slot = jnp.where(step // 2 == n, ORDER[n], slot)
        cp, ok = column_of(c, slot)
        main, any3, half3, _ = shape_of(r, cp)
        m, h = cp // 2, cp % 2
        full = main & (t == h)
        part = any3 & (t == half3)
        await_step(step)

        @pl.when(ok & (full | part))
        def _():
            ap_index = jnp.where(m == r, h, 2 + slot)
            rows = pl.ds(pl.multiple_of(t * HALF, HALF), HALF)
            left = jnp.concatenate([
                jnp.concatenate([pbuf[slot, t, 2 * g + 1], pbuf[slot, t, 2 * g]], axis=1) for g in range(2)
            ], axis=0)
            right = jnp.concatenate([
                jnp.concatenate([apbuf[ap_index, 1 - g], apbuf[ap_index, 3 - g]], axis=1) for g in range(2)
            ], axis=0)
            out_ref[rows, :] += lax.dot_general(
                left, right, (((0,), (0,)), ((), ())), preferred_element_type=jnp.float32
            )

        return carry

    lax.fori_loop(0, 2 * SLOTS, multiply, 0)
    for_roles(finish)


def on_device(prolong, applied, prolong_pattern, applied_pattern):
    return pl.pallas_call(
        kernel,
        out_shape=jax.ShapeDtypeStruct((prolong.shape[1], applied.shape[1]), jnp.float32),
        in_specs=[
            pl.BlockSpec(memory_space=pl.ANY),
            pl.BlockSpec(memory_space=pl.ANY),
            pl.BlockSpec(memory_space=pltpu.SMEM),
            pl.BlockSpec(memory_space=pltpu.SMEM),
        ],
        out_specs=pl.BlockSpec(memory_space=pltpu.VMEM),
        scratch_shapes=[
            pltpu.VMEM((SLOTS, 2, 4, GROUP, TILE), jnp.bfloat16),
            pltpu.VMEM((2 + SLOTS, 4, GROUP, TILE), jnp.bfloat16),
            pltpu.VMEM((MOST_SLABS, GROUP, TILE), jnp.bfloat16),
            pltpu.SemaphoreType.DMA((16,)),
            pltpu.SemaphoreType.DMA((MOST_SENDS,)),
            pltpu.SemaphoreType.DMA((SLOTS, 4)),
            pltpu.SemaphoreType.DMA((SLOTS, 2)),
            pltpu.SemaphoreType.DMA((MOST_RELAYED,)),
        ],
        compiler_params=pltpu.CompilerParams(
            collective_id=0, has_side_effects=True, vmem_limit_bytes=56000000
        ),
    )(prolong, applied, prolong_pattern.T, applied_pattern.T)


def solution(mesh):
    in_specs = (P("col", "row"), P("row", "col"), P("col", "row"), P("row", "col"))
    out_specs = P("row", "col")
    return jax.shard_map(
        on_device, mesh=mesh, in_specs=in_specs, out_specs=out_specs, check_vma=False
    )
```

```python
import collections

import jax
import jax.numpy as jnp
from jax import lax
from jax.experimental import pallas as pl
from jax.experimental.pallas import tpu as pltpu
from jax.sharding import PartitionSpec as P

MESH = pl.DeviceIdType.MESH
TILE = 128
ROWS = 8
COLS = 16
GROUP = 384
HALF = 256
FAR = 5
OWN = 2
SLOTS = 6
ORDER = (OWN, 1, 3, 0, 4, FAR)
SOURCE = -1
RELAY = 5
ACROSS = 6
EVERY = frozenset(range(4))

ROUTES = (
    (-1, 4, -1, 1, 1, -1, -1, 398, 49, 268, 125, 182, 346, 247, 12, 226, 191, 91, 0),
    (-1, -1, -1, 0, 1, -1, -1, 155, 201, 296, 195, 299, 39, 132, 52, 229, 235, 143, 0),
    (-1, 2, -1, -1, 2, 2, -1, 121, 380, 134, 460, 127, 147, 227, 97, 70, 178, 153, 0),
    (-1, 2, -1, -1, 1, 2, -1, 283, 405, 90, 124, 391, 475, 104, 122, 23, 242, 121, 0),
    (-1, 4, -1, -1, 1, -1, -1, 55, 238, 394, 341, 191, 72, 225, 108, 186, 243, 82, 0),
    (-1, -1, -1, 0, 0, 1, -1, 17, 138, 73, 122, 255, 222, 57, 60, 246, 213, 240, 0),
    (-1, -1, -1, 1, 1, -1, -1, 371, 3, 215, 408, 450, 114, 182, 14, 221, 208, 205, 0),
    (-1, -1, -1, 1, 1, -1, -1, 25, 444, 363, 316, 239, 446, 119, 133, 248, 250, 110, 0),
    (-1, 2, -1, -1, 2, 1, -1, 151, 330, 289, 88, 402, 145, 215, 150, 80, 184, 249, 0),
    (36, -1, 5, 5, 5, -1, -1, 53, 340, 21, 225, 404, 123, 20, 233, 163, 161, 94, 72),
    (-1, -1, -1, 1, 1, -1, -1, 419, 57, 302, 66, 211, 44, 95, 22, 139, 156, 50, 0),
    (-1, -1, -1, 0, 1, -1, -1, 361, 194, 80, 461, 421, 132, 48, 46, 131, 198, 96, 0),
    (-1, -1, -1, 3, -1, -1, -1, 407, 220, 462, 468, 386, 31, 41, 45, 222, 118, 42, 0),
    (-1, -1, -1, 1, 0, -1, -1, 16, 205, 389, 192, 387, 400, 5, 6, 89, 74, 63, 0),
    (17, 3, 5, 5, -1, 5, -1, 374, 242, 236, 113, 251, 7, 175, 154, 238, 56, 210, 36),
    (3, 5, 3, 3, -1, 5, -1, 12, 70, 279, 352, 139, 104, 112, 202, 207, 115, 69, 4),
    (44, -1, 5, 5, 5, -1, -1, 274, 347, 278, 150, 287, 29, 71, 245, 157, 183, 90, 53),
    (49, 5, -1, 1, 5, 5, -1, 237, 266, 275, 196, 92, 160, 137, 114, 217, 159, 212, 35),
    (-1, -1, -1, 1, 0, 1, -1, 11, 13, 227, 158, 365, 301, 16, 18, 123, 175, 219, 0),
    (35, 5, 5, 5, 5, 5, -1, 281, 94, 74, 300, 34, 101, 192, 174, 105, 166, 176, 33),
    (-1, -1, -1, 0, 1, 1, -1, 376, 226, 269, 2, 68, 5, 144, 73, 237, 199, 167, 0),
    (-1, -1, -1, 0, 0, 1, -1, 303, 318, 343, 459, 230, 258, 92, 142, 196, 230, 231, 0),
    (3, -1, 5, 0, -1, 5, -1, 252, 197, 317, 328, 89, 171, 47, 211, 147, 214, 172, 49),
    (-1, -1, 0, 0, 4, -1, -1, 107, 235, 286, 409, 137, 478, 9, 151, 93, 135, 43, 0),
    (-1, -1, -1, 0, 1, -1, -1, 43, 395, 62, 117, 456, 178, 68, 65, 189, 181, 125, 0),
    (-1, -1, -1, 3, -1, -1, -1, 438, 324, 248, 18, 382, 384, 134, 21, 117, 27, 55, 0),
    (-1, -1, -1, 0, -1, -1, -1, 165, 321, 441, 98, 297, 15, 24, 66, 138, 140, 83, 0),
    (-1, 1, -1, -1, 2, -1, -1, 75, 28, 272, 457, 186, 451, 113, 8, 46, 130, 40, 0),
    (-1, -1, -1, 0, 0, -1, -1, 377, 78, 166, 454, 472, 119, 32, 124, 162, 169, 87, 0),
    (-1, -1, -1, 1, -1, 0, -1, 474, 47, 379, 426, 443, 240, 59, 30, 107, 129, 203, 0),
    (19, -1, 5, -1, 2, -1, -1, 418, 33, 212, 216, 331, 97, 128, 220, 86, 190, 98, 77),
    (-1, -1, -1, 0, 1, 0, -1, 154, 280, 69, 440, 60, 106, 17, 44, 109, 171, 126, 0),
    (-1, -1, 0, -1, -1, -1, -1, 294, 50, 373, 473, 397, 204, 101, 180, 0, 0, 0, 0),
    (-1, -1, 0, -1, -1, -1, -1, 141, 45, 1, 221, 152, 67, 26, 99, 0, 0, 0, 0),
    (-1, 1, -1, -1, -1, -1, -1, 375, 229, 146, 108, 243, 403, 0, 75, 0, 0, 0, 0),
    (-1, -1, 0, -1, -1, -1, -1, 369, 333, 345, 87, 64, 120, 0, 164, 0, 0, 0, 0),
    (52, 5, 5, -1, -1, -1, -1, 61, 102, 188, 99, 359, 156, 218, 209, 0, 0, 0, 58),
    (12, 5, 5, -1, -1, -1, -1, 356, 95, 179, 430, 14, 479, 195, 228, 0, 0, 0, 116),
    (7, 5, 5, -1, -1, -1, -1, 455, 142, 290, 323, 412, 76, 0, 197, 0, 0, 0, 61),
    (-1, -1, -1, -1, -1, -1, -1, 445, 311, 383, 233, 372, 320, 0, 177, 0, 0, 0, 0),
    (-1, 1, -1, -1, -1, -1, -1, 52, 174, 393, 327, 170, 190, 206, 103, 0, 0, 0, 0),
    (11, 5, 5, -1, -1, -1, -1, 199, 288, 424, 173, 420, 381, 236, 223, 0, 0, 0, 127),
    (59, 5, 5, -1, -1, -1, -1, 411, 452, 309, 249, 59, 193, 0, 244, 0, 0, 0, 106),
    (-1, -1, -1, -1, -1, -1, -1, 86, 273, 40, 295, 465, 111, 0, 201, 0, 0, 0, 0),
    (6, 5, -1, -1, -1, -1, -1, 35, 334, 200, 232, 422, 223, 0, 136, 0, 0, 0, 0),
    (-1, -1, 0, -1, -1, -1, -1, 9, 183, 185, 135, 416, 149, 0, 39, 0, 0, 0, 0),
    (-1, -1, 0, -1, -1, -1, -1, 77, 161, 175, 22, 38, 458, 28, 145, 0, 0, 0, 0),
    (-1, 1, -1, -1, -1, -1, -1, 37, 159, 399, 82, 463, 332, 148, 38, 0, 0, 0, 0),
    (56, 5, -1, -1, -1, -1, -1, 84, 131, 367, 10, 276, 172, 0, 51, 0, 0, 0, 0),
    (-1, -1, 0, -1, -1, -1, -1, 344, 71, 105, 431, 93, 27, 0, 11, 0, 0, 0, 0),
    (8, 5, 5, -1, -1, -1, -1, 308, 439, 336, 4, 162, 360, 0, 10, 0, 0, 0, 1),
    (-1, 1, -1, -1, -1, -1, -1, 339, 467, 63, 133, 307, 23, 0, 2, 0, 0, 0, 0),
    (-1, -1, -1, -1, -1, -1, -1, 284, 432, 313, 51, 54, 388, 0, 232, 0, 0, 0, 0),
    (-1, -1, -1, -1, -1, -1, -1, 262, 414, 319, 103, 126, 250, 0, 152, 0, 0, 0, 0),
    (12, 5, 5, -1, -1, -1, -1, 214, 415, 36, 32, 364, 176, 155, 193, 0, 0, 0, 25),
    (4, 5, 5, -1, -1, -1, -1, 292, 315, 433, 58, 143, 410, 37, 85, 0, 0, 0, 7),
    (-1, -1, -1, -1, -1, -1, -1, 109, 253, 423, 206, 390, 169, 0, 234, 0, 0, 0, 0),
    (-1, -1, 0, -1, -1, -1, -1, 203, 401, 180, 476, 406, 41, 0, 251, 0, 0, 0, 0),
    (-1, 1, -1, -1, -1, -1, -1, 417, 228, 277, 118, 370, 0, 241, 168, 0, 0, 0, 0),
    (-1, 1, -1, -1, -1, -1, -1, 335, 79, 140, 428, 263, 453, 170, 78, 0, 0, 0, 0),
    (-1, 1, -1, -1, -1, -1, -1, 96, 314, 247, 181, 46, 231, 0, 239, 0, 0, 0, 0),
    (-1, -1, 0, -1, -1, -1, -1, 265, 189, 184, 293, 245, 168, 0, 141, 0, 0, 0, 0),
    (-1, -1, 0, -1, -1, -1, -1, 254, 129, 351, 282, 112, 271, 102, 200, 0, 0, 0, 0),
    (12, 5, 5, -1, -1, -1, -1, 471, 100, 83, 325, 413, 148, 185, 188, 0, 0, 0, 64),
    (-1, -1, 0, -1, -1, -1, -1, 305, 163, 208, 130, 202, 427, 0, 81, 0, 0, 0, 0),
    (-1, -1, -1, -1, -1, -1, -1, 270, 115, 164, 244, 310, 209, 0, 31, 0, 0, 0, 0),
    (-1, -1, 0, -1, -1, -1, -1, 354, 298, 264, 65, 217, 448, 84, 194, 0, 0, 0, 0),
    (12, 5, 5, -1, -1, -1, -1, 24, 116, 167, 466, 6, 19, 187, 173, 0, 0, 0, 29),
    (12, 5, 5, -1, -1, -1, -1, 30, 442, 207, 234, 348, 20, 100, 120, 0, 0, 0, 3),
    (12, 5, 5, -1, -1, -1, -1, 291, 285, 259, 261, 312, 48, 179, 146, 0, 0, 0, 15),
    (-1, -1, -1, -1, -1, -1, -1, 358, 429, 219, 322, 241, 368, 0, 76, 0, 0, 0, 0),
    (-1, 1, -1, -1, -1, -1, -1, 464, 213, 42, 470, 198, 437, 0, 19, 0, 0, 0, 0),
    (-1, -1, 0, -1, -1, -1, -1, 342, 91, 177, 434, 256, 425, 67, 158, 0, 0, 0, 0),
    (-1, -1, -1, -1, -1, -1, -1, 81, 85, 326, 477, 447, 355, 13, 34, 0, 0, 0, 0),
    (-1, -1, -1, -1, -1, -1, -1, 8, 136, 396, 392, 187, 449, 79, 149, 0, 0, 0, 0),
    (26, -1, 5, -1, -1, -1, -1, 362, 246, 338, 329, 257, 56, 165, 224, 0, 0, 0, 88),
    (-1, -1, -1, -1, -1, -1, -1, 144, 337, 353, 210, 224, 306, 54, 111, 0, 0, 0, 0),
    (-1, -1, -1, -1, -1, -1, -1, 385, 350, 218, 357, 26, 366, 216, 160, 0, 0, 0, 0),
    (-1, -1, 0, -1, -1, -1, -1, 436, 378, 128, 260, 349, 153, 0, 204, 0, 0, 0, 0),
    (-1, 1, -1, -1, -1, -1, -1, 267, 304, 469, 157, 110, 435, 0, 62, 0, 0, 0, 0),
)


def chip_of(device):
    return device[1] // 4, device[0] // 2, device[1] % 4


def role_of(device):
    x, y, z = chip_of(device)
    return (x - y) % 4, z, device[0] % 2


def p_kind(r, cp):
    m, h = cp // 2, cp % 2
    if m == r:
        return 0
    if (m == r + 1 and h == 0) or (m == r - 1 and h == 1):
        return 1
    return 2 if m == (r + 4) % ROWS else None


def p_pieces(kind, h):
    if kind == 0:
        return ((h, 0, 2, 0), (h, 2, 2, 1), (1 - h, 1 - h, 2, 2), (1 - h, 3 - h, 1, 3))
    half, start = (1 - h, h) if kind == 1 else (h, 0)
    return ((half, start, 2, 2), (half, start + 2, 1, 3))


def ap_pieces(slot):
    if slot == 4:
        return ((1, 2, 0), (3, 1, 1))
    return ((0, 2, 0), (2, 1 if slot in (0, FAR) else 2, 1))


def pieces():
    found = collections.OrderedDict()
    for r in range(ROWS):
        for cp in range(COLS):
            kind = p_kind(r, cp)
            if kind is None:
                continue
            z = cp % 4
            for n, (half, at, size, piece) in enumerate(p_pieces(kind, z % 2)):
                users = {n: (r, cp + d) for n, d in enumerate((-1, 1, -2, 2)) if 0 <= cp + d < COLS}
                users[4] = (r, (cp + 8) % COLS)
                entry = found.setdefault((0, kind, z, n), ((half, at, size, piece), []))
                entry[1].append(((r, cp), users))
    for r in range(ROWS):
        for c in range(COLS):
            for half in range(2):
                v = 2 * r + half - c
                slot = v + 2 if -2 <= v <= 2 else FAR if v in (8, -8) else None
                if slot is None:
                    continue
                x, y, z = chip_of((r, c))
                side = r - 1 + 2 * half
                for n, (at, size, piece) in enumerate(ap_pieces(slot)):
                    users = {1: ((r + 4) % ROWS, c)}
                    if 0 <= side < ROWS:
                        users[0 if side // 2 != r // 2 else ACROSS] = (side, c)
                    key = (1, r % 2, half, (x - y) % 4, z, n)
                    entry = found.setdefault(key, ((slot, half, at, size, piece), []))
                    entry[1].append(((r, c), users))
    return found


P_SLOT = (3, 1, 4, 0, FAR)

class Role:
    def __init__(self):
        self.sends = {}
        self.arrivals = {}
        self.greets = {}
        self.partners = {y: set() for y in range(4)}
        self.relayed = {}
        self.slabs = 0


def move_between(a, b):
    (ax, ay, _), (bx, by, bz) = chip_of(a), chip_of(b)
    return (bx - ax) % 4, (by - ay) % 4, bz, b[0] % 2


def make_plan():
    roles = {(a, z, core): Role() for a in range(4) for z in range(4) for core in range(2)}
    kinds = list(pieces().items())
    for n, (key, (_, instances)) in enumerate(kinds):
        size = kinds[n][1][0][3] if key[0] else kinds[n][1][0][2]
        offset, parents = ROUTES[n][0], ROUTES[n][1:7]
        for source, users in instances:
            place = dict(users)
            x, y, z = chip_of(source)
            if offset >= 0:
                rx, ry, rz = (x + offset % 4) % 4, (y + offset // 4 % 4) % 4, (z + offset // 16) % 4
                place[RELAY] = (2 * ry + source[0] % 2, 4 * rx + rz)
            place[SOURCE] = source
            reached = {SOURCE: SOURCE}
            edges = []

            def reach(node):
                if node in reached:
                    return reached[node]
                up = SOURCE if node == ACROSS else parents[node]
                if node not in place:
                    reached[node] = reach(up)
                    return reached[node]
                same = [u for u in users if node == RELAY and users[u] == place[RELAY]]
                if node == RELAY and place[RELAY] == source:
                    reached[node] = SOURCE
                    return SOURCE
                if same:
                    reached[same[0]] = same[0]
                    reached[node] = same[0]
                    edges.append((reach(up), same[0]))
                    return same[0]
                reached[node] = node
                edges.append((reach(up), node))
                return node

            if RELAY in place and RELAY in [parents[u] for u in users if u != ACROSS]:
                reach(RELAY)
            for user in users:
                reach(user)
            for a, b in edges:
                here, there = place[a], place[b]
                assert here != there
                mine, theirs = roles[role_of(here)], roles[role_of(there)]
                edge = (n, a, b, move_between(here, there))
                mine.sends.setdefault(edge, set()).add(here[0] // 2)
                theirs.arrivals.setdefault((n, b), set()).add(there[0] // 2)
                theirs.greets.setdefault(move_between(there, here), set()).add(there[0] // 2)
                mine.partners[here[0] // 2].add(there)
                if b == RELAY and n not in theirs.relayed:
                    theirs.relayed[n] = (theirs.slabs, len(theirs.relayed))
                    theirs.slabs += size
    return kinds, roles


KINDS, PLAN = make_plan()
MOST_SENDS = max(len(role.sends) for role in PLAN.values())
MOST_SLABS = max(max(role.slabs for role in PLAN.values()), 1)
MOST_RELAYED = max(max(len(role.relayed) for role in PLAN.values()), 1)


def target_role(role, move):
    return (role[0] + move[0] - move[1]) % 4, move[2], move[3]


def time_of(n, node):
    return -1 if node == ACROSS else ROUTES[n][13 + node]


def order_of_slots(role, member):
    latest = {slot: -1 for slot in ORDER}
    for (kind, node), members in PLAN[role].arrivals.items():
        if member in members and node != RELAY:
            key, (shape, _) = KINDS[kind]
            slot = shape[0] if key[0] else P_SLOT[node]
            latest[slot] = max(latest[slot], time_of(kind, node))
    return sum(slot * 8**n for n, slot in enumerate(sorted(ORDER, key=lambda slot: latest[slot])))


DIGITS = {(r, c): order_of_slots(role_of((r, c)), r // 2) for r in range(ROWS) for c in range(COLS)}


def column_of(c, slot):
    near = c + slot - 2
    far = slot == FAR
    cp = jnp.where(far, (c + 8) % COLS, near)
    return cp, far | ((near >= 0) & (near < COLS))


def shape_of(r, cp):
    m, h = cp // 2, cp % 2
    main = m == r
    low = (m == r + 1) & (h == 0)
    high = (m == r - 1) & (h == 1)
    far = m == (r + 4) % ROWS
    any3 = main | low | high | far
    half3 = jnp.where(far, h, 1 - h)
    start3 = jnp.where(main, 1 - h, jnp.where(high, 1, 0))
    return main, any3, half3, start3


def kernel(p_hbm, ap_hbm, pp_ref, app_ref, out_ref, pbuf, apbuf, relaybuf,
           load_sem, send_sem, precv, aprecv, relayrecv):
    r = lax.axis_index("row")
    c = lax.axis_index("col")
    x, y, z, core = c // 4, r // 2, c % 4, r % 2
    diagonal = (x - y + 4) % 4
    is_y = [y == n for n in range(4)]

    def for_members(members, act):
        if members == EVERY:
            act()
        elif members:
            test = None
            for n in sorted(members):
                test = is_y[n] if test is None else test | is_y[n]
            pl.when(test)(act)

    def for_roles(act):
        def for_z(a):
            for zz in range(4):
                def for_core(zz=zz):
                    for cc in range(2):
                        pl.when(core == cc)(lambda cc=cc: act((a, zz, cc)))
                pl.when(z == zz)(for_core)
        for a in range(4):
            pl.when(diagonal == a)(lambda a=a: for_z(a))

    def device(move):
        return 2 * ((y + move[1]) % 4) + move[3], 4 * ((x + move[0]) % 4) + move[2]

    def region(n, node, role):
        key, (shape, _) = KINDS[n]
        if node == RELAY:
            first, index = PLAN[role].relayed[n]
            size = shape[3] if key[0] else shape[2]
            return relaybuf.at[pl.ds(first, size)], relayrecv.at[index]
        if key[0] == 0:
            half, at, size, piece = shape
            slot = OWN if node == SOURCE else P_SLOT[node]
            return pbuf.at[slot, half, pl.ds(at, size)], precv.at[slot, piece]
        slot, half, at, size, piece = shape
        return apbuf.at[half if node == SOURCE else 2 + slot, pl.ds(at, size)], aprecv.at[slot, piece]

    def copy_of(role, edge):
        n, a, b, move = edge
        source, _ = region(n, a, role)
        target, recv = region(n, b, target_role(role, move))
        return pltpu.make_async_remote_copy(
            src_ref=source,
            dst_ref=target,
            send_sem=send_sem.at[list(PLAN[role].sends).index(edge)],
            recv_sem=recv,
            device_id=device(move),
            device_id_type=MESH,
        )

    def arrived(role, n, node):
        target, recv = region(n, node, role)
        pltpu.make_async_remote_copy(
            src_ref=target, dst_ref=target, send_sem=send_sem.at[0], recv_sem=recv,
            device_id=(r, c), device_id_type=MESH,
        ).wait_recv()

    def order_of(edge):
        n, _, b, _ = edge
        return -1 if b == ACROSS else ROUTES[n][7 + b]

    def passed_on(role):
        found = {}
        for (n, a, _, _), members in PLAN[role].sends.items():
            if a != SOURCE:
                found.setdefault((n, a), set()).update(members)
        return found

    barrier = pltpu.get_barrier_semaphore()

    def greet(role):
        for move, members in sorted(PLAN[role].greets.items()):
            for_members(members, lambda move=move: pl.semaphore_signal(
                barrier, inc=1, device_id=device(move), device_id_type=MESH))

    def send(role):
        plan = PLAN[role]
        counts = {}
        for n, partners in plan.partners.items():
            counts.setdefault(len(partners), set()).add(n)
        for count, members in counts.items():
            if count:
                for_members(members, lambda count=count: pl.semaphore_wait(barrier, count))
        for edge in sorted((e for e in plan.sends if e[1] == SOURCE), key=order_of):
            for_members(plan.sends[edge], lambda edge=edge: copy_of(role, edge).start())
        waits = sorted(passed_on(role).items(), key=lambda item: time_of(*item[0]))
        for (n, node), members in waits:
            for_members(members, lambda n=n, node=node: arrived(role, n, node))
            for edge in sorted((e for e in plan.sends if e[:2] == (n, node)), key=order_of):
                for_members(plan.sends[edge], lambda edge=edge: copy_of(role, edge).start())

    def finish(role):
        for edge, members in PLAN[role].sends.items():
            for_members(members, lambda edge=edge: copy_of(role, edge).wait_send())

    def await_step(step):
        def one(role):
            handed = passed_on(role)
            by_step = {}
            for (n, node), members in PLAN[role].arrivals.items():
                left = members - handed.get((n, node), set())
                if node == RELAY or not left:
                    continue
                key, (shape, _) = KINDS[n]
                at = 2 * shape[0] if key[0] else 2 * P_SLOT[node] + shape[0]
                by_step.setdefault(at, []).append((n, node, left))
            for at, waits in sorted(by_step.items()):
                @pl.when(step == at)
                def _():
                    for n, node, left in waits:
                        for_members(left, lambda n=n, node=node: arrived(role, n, node))

        for_roles(one)

    for_roles(greet)

    loads = []
    for g in range(2):
        for i in range(4):
            loads.append(pltpu.make_async_copy(
                p_hbm.at[pl.ds(g * GROUP, GROUP), pl.ds(i * TILE, TILE)],
                pbuf.at[OWN, i // 2, 2 * g + 1 - i % 2],
                load_sem.at[4 * g + i],
            ))
    for q in range(4):
        for j in range(2):
            loads.append(pltpu.make_async_copy(
                ap_hbm.at[pl.ds(q * GROUP, GROUP), pl.ds(j * TILE, TILE)],
                apbuf.at[q // 2, 2 * j + 1 - q % 2],
                load_sem.at[8 + 2 * q + j],
            ))
    for load in loads:
        load.start()
    for load in loads:
        load.wait()
    for a in range(6):
        g, rows = a // 3, pl.ds(a % 3 * TILE, TILE)
        for i in range(4):
            weight = pp_ref[i, a].astype(jnp.float32).astype(jnp.bfloat16)
            slab = (OWN, i // 2, 2 * g + 1 - i % 2, rows)
            pbuf[slab] = pbuf[slab] * weight
    for a in range(12):
        q, rows = a // 3, pl.ds(a % 3 * TILE, TILE)
        for j in range(2):
            weight = app_ref[j, a].astype(jnp.float32).astype(jnp.bfloat16)
            slab = (q // 2, 2 * j + 1 - q % 2, rows)
            apbuf[slab] = apbuf[slab] * weight

    for_roles(send)

    blank = jnp.zeros((GROUP, TILE), jnp.bfloat16)
    apbuf[2 + 0, 3] = blank
    apbuf[2 + 4, 0] = blank
    apbuf[2 + FAR, 3] = blank
    for slot in range(SLOTS):
        if slot != OWN:
            cp, ok = column_of(c, slot)
            _, any3, half, start = shape_of(r, cp)

            @pl.when(ok & any3)
            def _():
                pbuf[slot, half, jnp.where(start == 0, 3, 0)] = blank
    out_ref[...] = jnp.zeros_like(out_ref)

    number = r * COLS + c
    usual = collections.Counter(DIGITS.values()).most_common(1)[0][0]
    digits = jnp.int32(usual)
    for (row, col), order in DIGITS.items():
        if order != usual:
            digits = jnp.where(number == row * COLS + col, order, digits)

    def multiply(step, digits):
        t = step % 2
        slot = digits % 8
        cp, ok = column_of(c, slot)
        main, any3, half3, _ = shape_of(r, cp)
        m, h = cp // 2, cp % 2
        full = main & (t == h)
        part = any3 & (t == half3)
        await_step(2 * slot + t)

        @pl.when(ok & (full | part))
        def _():
            ap_index = jnp.where(m == r, h, 2 + slot)
            rows = pl.ds(pl.multiple_of(t * HALF, HALF), HALF)
            left = jnp.concatenate([
                jnp.concatenate([pbuf[slot, t, 2 * g + 1], pbuf[slot, t, 2 * g]], axis=1) for g in range(2)
            ], axis=0)
            right = jnp.concatenate([
                jnp.concatenate([apbuf[ap_index, 1 - g], apbuf[ap_index, 3 - g]], axis=1) for g in range(2)
            ], axis=0)
            out_ref[rows, :] += lax.dot_general(
                left, right, (((0,), (0,)), ((), ())), preferred_element_type=jnp.float32
            )

        return jnp.where(t == 1, digits // 8, digits)

    lax.fori_loop(0, 2 * SLOTS, multiply, digits)
    for_roles(finish)


def on_device(prolong, applied, prolong_pattern, applied_pattern):
    return pl.pallas_call(
        kernel,
        out_shape=jax.ShapeDtypeStruct((prolong.shape[1], applied.shape[1]), jnp.float32),
        in_specs=[
            pl.BlockSpec(memory_space=pl.ANY),
            pl.BlockSpec(memory_space=pl.ANY),
            pl.BlockSpec(memory_space=pltpu.SMEM),
            pl.BlockSpec(memory_space=pltpu.SMEM),
        ],
        out_specs=pl.BlockSpec(memory_space=pltpu.VMEM),
        scratch_shapes=[
            pltpu.VMEM((SLOTS, 2, 4, GROUP, TILE), jnp.bfloat16),
            pltpu.VMEM((2 + SLOTS, 4, GROUP, TILE), jnp.bfloat16),
            pltpu.VMEM((MOST_SLABS, GROUP, TILE), jnp.bfloat16),
            pltpu.SemaphoreType.DMA((16,)),
            pltpu.SemaphoreType.DMA((MOST_SENDS,)),
            pltpu.SemaphoreType.DMA((SLOTS, 4)),
            pltpu.SemaphoreType.DMA((SLOTS, 2)),
            pltpu.SemaphoreType.DMA((MOST_RELAYED,)),
        ],
        compiler_params=pltpu.CompilerParams(
            collective_id=0, has_side_effects=True, vmem_limit_bytes=56000000
        ),
    )(prolong, applied, prolong_pattern.T, applied_pattern.T)


def solution(mesh):
    in_specs = (P("col", "row"), P("row", "col"), P("col", "row"), P("row", "col"))
    out_specs = P("row", "col")
    return jax.shard_map(
        on_device, mesh=mesh, in_specs=in_specs, out_specs=out_specs, check_vma=False
    )
```

```python
import collections

import jax
import jax.numpy as jnp
from jax import lax
from jax.experimental import pallas as pl
from jax.experimental.pallas import tpu as pltpu
from jax.sharding import PartitionSpec as P

MESH = pl.DeviceIdType.MESH
TILE = 128
ROWS = 8
COLS = 16
GROUP = 384
HALF = 256
FAR = 5
OWN = 2
SLOTS = 6
ORDER = (OWN, 1, 3, 0, 4, FAR)
SOURCE = -1
RELAY = 5
ACROSS = 6
EVERY = frozenset(range(4))

ROUTES = (
    (-1, -1, -1, 0, 1, 0, -1, 21, 5, 3, 438, 60, 217, 41, 18, 194, 170, 138, 0),
    (-1, 1, -1, -1, 1, -1, -1, 289, 322, 220, 304, 295, 223, 246, 131, 165, 240, 149, 0),
    (-1, 1, -1, 4, 1, -1, -1, 288, 43, 406, 154, 118, 374, 232, 64, 220, 216, 81, 0),
    (17, 3, 5, 5, -1, 5, -1, 472, 457, 151, 313, 200, 56, 233, 97, 155, 107, 128, 20),
    (-1, -1, -1, -1, 2, -1, -1, 196, 18, 85, 299, 440, 26, 196, 50, 142, 236, 126, 0),
    (-1, -1, -1, 1, 0, -1, -1, 32, 306, 192, 319, 479, 237, 120, 112, 241, 234, 204, 0),
    (17, -1, 5, 5, 0, 0, -1, 16, 397, 214, 159, 2, 369, 52, 186, 214, 197, 227, 73),
    (7, -1, 3, 3, -1, 5, -1, 241, 386, 1, 137, 41, 64, 218, 239, 243, 180, 136, 26),
    (-1, 2, -1, -1, 2, 1, -1, 318, 250, 62, 112, 282, 403, 181, 151, 78, 201, 242, 0),
    (35, -1, 5, 5, 5, 5, -1, 401, 38, 328, 461, 274, 87, 21, 148, 133, 162, 150, 37),
    (-1, -1, -1, -1, 2, -1, -1, 358, 31, 183, 290, 127, 24, 159, 24, 130, 211, 62, 0),
    (-1, -1, -1, 1, -1, -1, -1, 293, 372, 197, 82, 80, 187, 103, 83, 173, 61, 15, 0),
    (-1, -1, -1, 0, 1, -1, -1, 207, 188, 25, 59, 149, 202, 23, 11, 210, 118, 14, 0),
    (-1, -1, -1, 1, 1, -1, -1, 102, 269, 364, 294, 199, 99, 4, 27, 116, 147, 48, 0),
    (-1, -1, -1, 4, 1, -1, -1, 86, 83, 257, 49, 420, 445, 8, 7, 183, 235, 28, 0),
    (-1, -1, -1, 4, 4, -1, -1, 271, 246, 194, 19, 71, 253, 33, 31, 100, 99, 3, 0),
    (35, -1, -1, 5, 4, -1, -1, 477, 352, 272, 76, 39, 266, 166, 176, 192, 217, 55, 91),
    (-1, -1, -1, 1, 0, -1, -1, 89, 162, 424, 28, 402, 210, 34, 47, 163, 169, 213, 0),
    (-1, -1, 4, 3, -1, -1, -1, 431, 362, 380, 6, 388, 171, 110, 247, 167, 42, 152, 0),
    (-1, -1, -1, 1, 0, -1, -1, 359, 191, 463, 446, 404, 130, 59, 89, 182, 206, 238, 0),
    (3, -1, -1, 0, -1, 5, -1, 165, 427, 176, 436, 42, 273, 36, 159, 208, 228, 185, 72),
    (-1, -1, -1, 1, 1, 1, -1, 270, 423, 175, 226, 116, 370, 119, 98, 203, 226, 189, 0),
    (44, -1, 5, 5, 4, -1, -1, 470, 321, 378, 320, 114, 139, 199, 222, 174, 177, 46, 75),
    (-1, -1, 4, 0, 4, -1, -1, 184, 218, 333, 145, 384, 235, 70, 224, 231, 212, 102, 0),
    (48, 5, -1, 5, -1, -1, -1, 344, 455, 74, 393, 327, 126, 171, 168, 178, 125, 93, 29),
    (-1, -1, -1, 3, -1, -1, -1, 92, 287, 133, 11, 169, 78, 17, 54, 104, 35, 39, 0),
    (-1, -1, 2, -1, 2, -1, -1, 260, 347, 224, 30, 382, 395, 49, 140, 44, 153, 68, 0),
    (-1, 1, -1, -1, 1, -1, -1, 166, 315, 351, 182, 256, 157, 157, 63, 106, 172, 22, 0),
    (-1, -1, -1, -1, 2, -1, -1, 468, 449, 476, 221, 70, 117, 58, 122, 108, 215, 59, 0),
    (-1, 2, -1, -1, 2, -1, -1, 168, 434, 0, 227, 466, 57, 114, 65, 38, 144, 101, 0),
    (-1, -1, -1, -1, 2, 0, -1, 350, 88, 280, 150, 456, 381, 96, 94, 85, 184, 229, 0),
    (-1, -1, -1, -1, 2, -1, -1, 452, 412, 408, 267, 433, 209, 146, 134, 139, 219, 90, 0),
    (-1, 1, -1, -1, -1, -1, -1, 4, 138, 447, 142, 426, 101, 145, 40, 0, 0, 0, 0),
    (-1, 1, -1, -1, -1, -1, -1, 95, 213, 232, 54, 123, 259, 193, 84, 0, 0, 0, 0),
    (-1, 1, -1, -1, -1, -1, -1, 249, 360, 238, 100, 55, 281, 0, 129, 0, 0, 0, 0),
    (-1, 1, -1, -1, -1, -1, -1, 285, 385, 409, 373, 262, 234, 0, 195, 0, 0, 0, 0),
    (-1, -1, -1, -1, -1, -1, -1, 469, 245, 153, 462, 65, 314, 175, 154, 0, 0, 0, 0),
    (-1, -1, 0, -1, -1, -1, -1, 375, 186, 212, 410, 411, 179, 123, 209, 0, 0, 0, 0),
    (4, 5, 5, -1, -1, -1, -1, 275, 185, 204, 105, 416, 233, 0, 221, 0, 0, 0, 115),
    (52, -1, 5, -1, -1, -1, -1, 301, 464, 181, 140, 8, 180, 0, 202, 0, 0, 0, 77),
    (12, 5, 5, -1, -1, -1, -1, 12, 144, 444, 276, 278, 297, 160, 205, 0, 0, 0, 86),
    (12, 5, 5, -1, -1, -1, -1, 219, 136, 195, 300, 361, 147, 69, 92, 0, 0, 0, 13),
    (-1, -1, -1, -1, -1, -1, -1, 465, 417, 251, 228, 104, 435, 0, 225, 0, 0, 0, 0),
    (-1, 1, -1, -1, -1, -1, -1, 242, 376, 239, 52, 132, 448, 0, 135, 0, 0, 0, 0),
    (-1, -1, 0, -1, -1, -1, -1, 310, 261, 173, 474, 336, 244, 0, 124, 0, 0, 0, 0),
    (4, -1, 5, -1, -1, -1, -1, 96, 216, 46, 170, 399, 243, 0, 132, 0, 0, 0, 25),
    (-1, -1, -1, -1, -1, -1, -1, 108, 205, 343, 467, 342, 383, 57, 105, 0, 0, 0, 0),
    (-1, -1, -1, -1, -1, -1, -1, 91, 109, 292, 164, 141, 79, 12, 53, 0, 0, 0, 0),
    (-1, 1, -1, -1, -1, -1, -1, 346, 35, 34, 247, 307, 429, 0, 19, 0, 0, 0, 0),
    (-1, 1, -1, -1, -1, -1, -1, 53, 340, 44, 279, 124, 330, 0, 45, 0, 0, 0, 0),
    (-1, -1, 0, -1, -1, -1, -1, 371, 451, 67, 428, 206, 120, 0, 6, 0, 0, 0, 0),
    (-1, 1, -1, -1, -1, -1, -1, 215, 10, 312, 400, 45, 143, 0, 1, 0, 0, 0, 0),
    (12, -1, 5, -1, -1, -1, -1, 113, 459, 33, 430, 121, 283, 0, 198, 0, 0, 0, 67),
    (4, -1, 5, -1, -1, -1, -1, 419, 236, 338, 189, 40, 324, 0, 111, 0, 0, 0, 16),
    (12, 5, 5, -1, -1, -1, -1, 354, 72, 255, 389, 134, 81, 141, 95, 0, 0, 0, 5),
    (-1, 1, -1, -1, -1, -1, -1, 337, 163, 335, 296, 268, 305, 74, 10, 0, 0, 0, 0),
    (57, 5, 5, -1, -1, -1, -1, 390, 291, 356, 379, 309, 316, 0, 237, 0, 0, 0, 127),
    (-1, -1, 0, -1, -1, -1, -1, 36, 367, 203, 363, 106, 13, 0, 187, 0, 0, 0, 0),
    (-1, 1, -1, -1, -1, -1, -1, 394, 190, 50, 58, 284, 355, 158, 56, 0, 0, 0, 0),
    (4, 5, 5, -1, -1, -1, -1, 61, 298, 29, 345, 17, 323, 143, 191, 0, 0, 0, 82),
    (-1, -1, -1, -1, -1, -1, -1, 94, 348, 172, 263, 413, 231, 0, 230, 0, 0, 0, 0),
    (-1, -1, 0, -1, -1, -1, -1, 471, 407, 27, 454, 473, 329, 0, 244, 0, 0, 0, 0),
    (-1, 1, -1, -1, -1, -1, -1, 158, 211, 339, 90, 225, 155, 245, 188, 0, 0, 0, 0),
    (-1, 1, -1, -1, -1, -1, -1, 334, 152, 240, 331, 332, 7, 200, 109, 0, 0, 0, 0),
    (-1, -1, 0, -1, -1, -1, -1, 37, 265, 14, 51, 422, 366, 0, 133, 0, 0, 0, 0),
    (-1, -1, -1, -1, -1, -1, -1, 148, 398, 110, 377, 73, 418, 0, 161, 0, 0, 0, 0),
    (-1, -1, -1, -1, -1, -1, -1, 432, 167, 405, 302, 15, 122, 156, 41, 0, 0, 0, 0),
    (-1, 1, -1, -1, -1, -1, -1, 47, 198, 115, 349, 161, 68, 190, 87, 0, 0, 0, 0),
    (-1, -1, 0, -1, -1, -1, -1, 421, 303, 392, 146, 443, 208, 9, 179, 0, 0, 0, 0),
    (12, 5, 5, -1, -1, -1, -1, 23, 326, 258, 387, 69, 450, 71, 66, 0, 0, 0, 2),
    (55, 5, -1, -1, -1, -1, -1, 177, 131, 201, 391, 475, 252, 0, 51, 0, 0, 0, 0),
    (-1, 1, -1, -1, -1, -1, -1, 353, 317, 396, 156, 478, 414, 0, 80, 0, 0, 0, 0),
    (-1, -1, -1, -1, -1, -1, -1, 439, 442, 222, 425, 248, 437, 79, 117, 0, 0, 0, 0),
    (-1, -1, -1, -1, -1, -1, -1, 308, 66, 77, 357, 75, 254, 32, 30, 0, 0, 0, 0),
    (-1, -1, -1, -1, -1, -1, -1, 48, 460, 22, 129, 160, 174, 76, 121, 0, 0, 0, 0),
    (-1, 1, -1, -1, -1, -1, -1, 368, 20, 63, 341, 97, 286, 113, 43, 0, 0, 0, 0),
    (-1, -1, -1, -1, -1, -1, -1, 441, 111, 98, 84, 365, 135, 223, 137, 0, 0, 0, 0),
    (-1, -1, -1, -1, -1, -1, -1, 93, 264, 325, 277, 229, 128, 60, 207, 0, 0, 0, 0),
    (-1, -1, -1, -1, -1, -1, -1, 9, 103, 453, 415, 107, 458, 0, 88, 0, 0, 0, 0),
    (-1, 1, -1, -1, -1, -1, -1, 193, 178, 119, 230, 125, 311, 0, 164, 0, 0, 0, 0),
)


def chip_of(device):
    return device[1] // 4, device[0] // 2, device[1] % 4


def role_of(device):
    x, y, z = chip_of(device)
    return (x - y) % 4, z, device[0] % 2


def p_kind(r, cp):
    m, h = cp // 2, cp % 2
    if m == r:
        return 0
    if (m == r + 1 and h == 0) or (m == r - 1 and h == 1):
        return 1
    return 2 if m == (r + 4) % ROWS else None


def p_pieces(kind, h):
    if kind == 0:
        return ((h, 0, 2, 0), (h, 2, 2, 1), (1 - h, 1 - h, 2, 2), (1 - h, 3 - h, 1, 3))
    half, start = (1 - h, h) if kind == 1 else (h, 0)
    return ((half, start, 2, 2), (half, start + 2, 1, 3))


def ap_pieces(slot):
    if slot == 4:
        return ((1, 2, 0), (3, 1, 1))
    return ((0, 2, 0), (2, 1 if slot in (0, FAR) else 2, 1))


def pieces():
    found = collections.OrderedDict()
    for r in range(ROWS):
        for cp in range(COLS):
            kind = p_kind(r, cp)
            if kind is None:
                continue
            z = cp % 4
            for n, (half, at, size, piece) in enumerate(p_pieces(kind, z % 2)):
                users = {n: (r, cp + d) for n, d in enumerate((-1, 1, -2, 2)) if 0 <= cp + d < COLS}
                users[4] = (r, (cp + 8) % COLS)
                entry = found.setdefault((0, kind, z, n), ((half, at, size, piece), []))
                entry[1].append(((r, cp), users))
    for r in range(ROWS):
        for c in range(COLS):
            for half in range(2):
                v = 2 * r + half - c
                slot = v + 2 if -2 <= v <= 2 else FAR if v in (8, -8) else None
                if slot is None:
                    continue
                x, y, z = chip_of((r, c))
                side = r - 1 + 2 * half
                for n, (at, size, piece) in enumerate(ap_pieces(slot)):
                    users = {1: ((r + 4) % ROWS, c)}
                    if 0 <= side < ROWS:
                        users[0 if side // 2 != r // 2 else ACROSS] = (side, c)
                    key = (1, r % 2, half, (x - y) % 4, z, n)
                    entry = found.setdefault(key, ((slot, half, at, size, piece), []))
                    entry[1].append(((r, c), users))
    return found


P_SLOT = (3, 1, 4, 0, FAR)

class Role:
    def __init__(self):
        self.sends = {}
        self.arrivals = {}
        self.greets = {}
        self.partners = {y: set() for y in range(4)}
        self.relayed = {}
        self.slabs = 0


def move_between(a, b):
    (ax, ay, _), (bx, by, bz) = chip_of(a), chip_of(b)
    return (bx - ax) % 4, (by - ay) % 4, bz, b[0] % 2


def make_plan():
    roles = {(a, z, core): Role() for a in range(4) for z in range(4) for core in range(2)}
    kinds = list(pieces().items())
    for n, (key, (_, instances)) in enumerate(kinds):
        size = kinds[n][1][0][3] if key[0] else kinds[n][1][0][2]
        offset, parents = ROUTES[n][0], ROUTES[n][1:7]
        for source, users in instances:
            place = dict(users)
            x, y, z = chip_of(source)
            if offset >= 0:
                rx, ry, rz = (x + offset % 4) % 4, (y + offset // 4 % 4) % 4, (z + offset // 16) % 4
                place[RELAY] = (2 * ry + source[0] % 2, 4 * rx + rz)
            place[SOURCE] = source
            reached = {SOURCE: SOURCE}
            edges = []

            def reach(node):
                if node in reached:
                    return reached[node]
                up = SOURCE if node == ACROSS else parents[node]
                if node not in place:
                    reached[node] = reach(up)
                    return reached[node]
                same = [u for u in users if node == RELAY and users[u] == place[RELAY]]
                if node == RELAY and place[RELAY] == source:
                    reached[node] = SOURCE
                    return SOURCE
                if same:
                    reached[same[0]] = same[0]
                    reached[node] = same[0]
                    edges.append((reach(up), same[0]))
                    return same[0]
                reached[node] = node
                edges.append((reach(up), node))
                return node

            if RELAY in place and RELAY in [parents[u] for u in users if u != ACROSS]:
                reach(RELAY)
            for user in users:
                reach(user)
            for a, b in edges:
                here, there = place[a], place[b]
                assert here != there
                mine, theirs = roles[role_of(here)], roles[role_of(there)]
                edge = (n, a, b, move_between(here, there))
                mine.sends.setdefault(edge, set()).add(here[0] // 2)
                theirs.arrivals.setdefault((n, b), set()).add(there[0] // 2)
                theirs.greets.setdefault(move_between(there, here), set()).add(there[0] // 2)
                mine.partners[here[0] // 2].add(there)
                if b == RELAY and n not in theirs.relayed:
                    theirs.relayed[n] = (theirs.slabs, len(theirs.relayed))
                    theirs.slabs += size
    return kinds, roles


KINDS, PLAN = make_plan()
MOST_SENDS = max(len(role.sends) for role in PLAN.values())
MOST_SLABS = max(max(role.slabs for role in PLAN.values()), 1)
MOST_RELAYED = max(max(len(role.relayed) for role in PLAN.values()), 1)


def target_role(role, move):
    return (role[0] + move[0] - move[1]) % 4, move[2], move[3]


def time_of(n, node):
    return -1 if node == ACROSS else ROUTES[n][13 + node]


def order_of_slots(role, member):
    latest = {slot: -1 for slot in ORDER}
    for (kind, node), members in PLAN[role].arrivals.items():
        if member in members and node != RELAY:
            key, (shape, _) = KINDS[kind]
            slot = shape[0] if key[0] else P_SLOT[node]
            latest[slot] = max(latest[slot], time_of(kind, node))
    return sum(slot * 8**n for n, slot in enumerate(sorted(ORDER, key=lambda slot: latest[slot])))


DIGITS = {(r, c): order_of_slots(role_of((r, c)), r // 2) for r in range(ROWS) for c in range(COLS)}


def column_of(c, slot):
    near = c + slot - 2
    far = slot == FAR
    cp = jnp.where(far, (c + 8) % COLS, near)
    return cp, far | ((near >= 0) & (near < COLS))


def shape_of(r, cp):
    m, h = cp // 2, cp % 2
    main = m == r
    low = (m == r + 1) & (h == 0)
    high = (m == r - 1) & (h == 1)
    far = m == (r + 4) % ROWS
    any3 = main | low | high | far
    half3 = jnp.where(far, h, 1 - h)
    start3 = jnp.where(main, 1 - h, jnp.where(high, 1, 0))
    return main, any3, half3, start3


def kernel(p_hbm, ap_hbm, pp_ref, app_ref, out_ref, pbuf, apbuf, relaybuf,
           load_sem, send_sem, precv, aprecv, relayrecv):
    r = lax.axis_index("row")
    c = lax.axis_index("col")
    x, y, z, core = c // 4, r // 2, c % 4, r % 2
    diagonal = (x - y + 4) % 4
    is_y = [y == n for n in range(4)]

    def for_members(members, act):
        if members == EVERY:
            act()
        elif members:
            test = None
            for n in sorted(members):
                test = is_y[n] if test is None else test | is_y[n]
            pl.when(test)(act)

    def for_roles(act):
        def for_z(a):
            for zz in range(4):
                def for_core(zz=zz):
                    for cc in range(2):
                        pl.when(core == cc)(lambda cc=cc: act((a, zz, cc)))
                pl.when(z == zz)(for_core)
        for a in range(4):
            pl.when(diagonal == a)(lambda a=a: for_z(a))

    def device(move):
        return 2 * ((y + move[1]) % 4) + move[3], 4 * ((x + move[0]) % 4) + move[2]

    def region(n, node, role):
        key, (shape, _) = KINDS[n]
        if node == RELAY:
            first, index = PLAN[role].relayed[n]
            size = shape[3] if key[0] else shape[2]
            return relaybuf.at[pl.ds(first, size)], relayrecv.at[index]
        if key[0] == 0:
            half, at, size, piece = shape
            slot = OWN if node == SOURCE else P_SLOT[node]
            return pbuf.at[slot, half, pl.ds(at, size)], precv.at[slot, piece]
        slot, half, at, size, piece = shape
        return apbuf.at[half if node == SOURCE else 2 + slot, pl.ds(at, size)], aprecv.at[slot, piece]

    def copy_of(role, edge):
        n, a, b, move = edge
        source, _ = region(n, a, role)
        target, recv = region(n, b, target_role(role, move))
        return pltpu.make_async_remote_copy(
            src_ref=source,
            dst_ref=target,
            send_sem=send_sem.at[list(PLAN[role].sends).index(edge)],
            recv_sem=recv,
            device_id=device(move),
            device_id_type=MESH,
        )

    def arrived(role, n, node):
        target, recv = region(n, node, role)
        pltpu.make_async_remote_copy(
            src_ref=target, dst_ref=target, send_sem=send_sem.at[0], recv_sem=recv,
            device_id=(r, c), device_id_type=MESH,
        ).wait_recv()

    def order_of(edge):
        n, _, b, _ = edge
        return -1 if b == ACROSS else ROUTES[n][7 + b]

    def passed_on(role):
        found = {}
        for (n, a, _, _), members in PLAN[role].sends.items():
            if a != SOURCE:
                found.setdefault((n, a), set()).update(members)
        return found

    barrier = pltpu.get_barrier_semaphore()

    def greet(role):
        for move, members in sorted(PLAN[role].greets.items()):
            for_members(members, lambda move=move: pl.semaphore_signal(
                barrier, inc=1, device_id=device(move), device_id_type=MESH))

    def send(role):
        plan = PLAN[role]
        counts = {}
        for n, partners in plan.partners.items():
            counts.setdefault(len(partners), set()).add(n)
        for count, members in counts.items():
            if count:
                for_members(members, lambda count=count: pl.semaphore_wait(barrier, count))
        for edge in sorted((e for e in plan.sends if e[1] == SOURCE), key=order_of):
            for_members(plan.sends[edge], lambda edge=edge: copy_of(role, edge).start())
        waits = sorted(passed_on(role).items(), key=lambda item: time_of(*item[0]))
        for (n, node), members in waits:
            for_members(members, lambda n=n, node=node: arrived(role, n, node))
            for edge in sorted((e for e in plan.sends if e[:2] == (n, node)), key=order_of):
                for_members(plan.sends[edge], lambda edge=edge: copy_of(role, edge).start())

    def finish(role):
        for edge, members in PLAN[role].sends.items():
            for_members(members, lambda edge=edge: copy_of(role, edge).wait_send())

    def await_step(step):
        def one(role):
            handed = passed_on(role)
            by_step = {}
            for (n, node), members in PLAN[role].arrivals.items():
                left = members - handed.get((n, node), set())
                if node == RELAY or not left:
                    continue
                key, (shape, _) = KINDS[n]
                at = 2 * shape[0] if key[0] else 2 * P_SLOT[node] + shape[0]
                by_step.setdefault(at, []).append((n, node, left))
            for at, waits in sorted(by_step.items()):
                @pl.when(step == at)
                def _():
                    for n, node, left in waits:
                        for_members(left, lambda n=n, node=node: arrived(role, n, node))

        for_roles(one)

    for_roles(greet)

    loads = []
    for g in range(2):
        for i in range(4):
            loads.append(pltpu.make_async_copy(
                p_hbm.at[pl.ds(g * GROUP, GROUP), pl.ds(i * TILE, TILE)],
                pbuf.at[OWN, i // 2, 2 * g + 1 - i % 2],
                load_sem.at[4 * g + i],
            ))
    for q in range(4):
        for j in range(2):
            loads.append(pltpu.make_async_copy(
                ap_hbm.at[pl.ds(q * GROUP, GROUP), pl.ds(j * TILE, TILE)],
                apbuf.at[q // 2, 2 * j + 1 - q % 2],
                load_sem.at[8 + 2 * q + j],
            ))
    for load in loads:
        load.start()
    for load in loads:
        load.wait()
    for a in range(6):
        g, rows = a // 3, pl.ds(a % 3 * TILE, TILE)
        for i in range(4):
            weight = pp_ref[i, a].astype(jnp.float32).astype(jnp.bfloat16)
            slab = (OWN, i // 2, 2 * g + 1 - i % 2, rows)
            pbuf[slab] = pbuf[slab] * weight
    for a in range(12):
        q, rows = a // 3, pl.ds(a % 3 * TILE, TILE)
        for j in range(2):
            weight = app_ref[j, a].astype(jnp.float32).astype(jnp.bfloat16)
            slab = (q // 2, 2 * j + 1 - q % 2, rows)
            apbuf[slab] = apbuf[slab] * weight

    for_roles(send)

    blank = jnp.zeros((GROUP, TILE), jnp.bfloat16)
    apbuf[2 + 0, 3] = blank
    apbuf[2 + 4, 0] = blank
    apbuf[2 + FAR, 3] = blank
    for slot in range(SLOTS):
        if slot != OWN:
            cp, ok = column_of(c, slot)
            _, any3, half, start = shape_of(r, cp)

            @pl.when(ok & any3)
            def _():
                pbuf[slot, half, jnp.where(start == 0, 3, 0)] = blank
    out_ref[...] = jnp.zeros_like(out_ref)

    number = r * COLS + c
    usual = collections.Counter(DIGITS.values()).most_common(1)[0][0]
    digits = jnp.int32(usual)
    for (row, col), order in DIGITS.items():
        if order != usual:
            digits = jnp.where(number == row * COLS + col, order, digits)

    def multiply(step, digits):
        t = step % 2
        slot = digits % 8
        cp, ok = column_of(c, slot)
        main, any3, half3, _ = shape_of(r, cp)
        m, h = cp // 2, cp % 2
        full = main & (t == h)
        part = any3 & (t == half3)
        await_step(2 * slot + t)

        @pl.when(ok & (full | part))
        def _():
            ap_index = jnp.where(m == r, h, 2 + slot)
            rows = pl.ds(pl.multiple_of(t * HALF, HALF), HALF)
            left = jnp.concatenate([
                jnp.concatenate([pbuf[slot, t, 2 * g + 1], pbuf[slot, t, 2 * g]], axis=1) for g in range(2)
            ], axis=0)
            right = jnp.concatenate([
                jnp.concatenate([apbuf[ap_index, 1 - g], apbuf[ap_index, 3 - g]], axis=1) for g in range(2)
            ], axis=0)
            out_ref[rows, :] += lax.dot_general(
                left, right, (((0,), (0,)), ((), ())), preferred_element_type=jnp.float32
            )

        return jnp.where(t == 1, digits // 8, digits)

    lax.fori_loop(0, 2 * SLOTS, multiply, digits)
    for_roles(finish)


def on_device(prolong, applied, prolong_pattern, applied_pattern):
    return pl.pallas_call(
        kernel,
        out_shape=jax.ShapeDtypeStruct((prolong.shape[1], applied.shape[1]), jnp.float32),
        in_specs=[
            pl.BlockSpec(memory_space=pl.ANY),
            pl.BlockSpec(memory_space=pl.ANY),
            pl.BlockSpec(memory_space=pltpu.SMEM),
            pl.BlockSpec(memory_space=pltpu.SMEM),
        ],
        out_specs=pl.BlockSpec(memory_space=pltpu.VMEM),
        scratch_shapes=[
            pltpu.VMEM((SLOTS, 2, 4, GROUP, TILE), jnp.bfloat16),
            pltpu.VMEM((2 + SLOTS, 4, GROUP, TILE), jnp.bfloat16),
            pltpu.VMEM((MOST_SLABS, GROUP, TILE), jnp.bfloat16),
            pltpu.SemaphoreType.DMA((16,)),
            pltpu.SemaphoreType.DMA((MOST_SENDS,)),
            pltpu.SemaphoreType.DMA((SLOTS, 4)),
            pltpu.SemaphoreType.DMA((SLOTS, 2)),
            pltpu.SemaphoreType.DMA((MOST_RELAYED,)),
        ],
        compiler_params=pltpu.CompilerParams(
            collective_id=0, has_side_effects=True, vmem_limit_bytes=56000000
        ),
    )(prolong, applied, prolong_pattern.T, applied_pattern.T)


def solution(mesh):
    in_specs = (P("col", "row"), P("row", "col"), P("col", "row"), P("row", "col"))
    out_specs = P("row", "col")
    return jax.shard_map(
        on_device, mesh=mesh, in_specs=in_specs, out_specs=out_specs, check_vma=False
    )
```

```python
import collections

import jax
import jax.numpy as jnp
from jax import lax
from jax.experimental import pallas as pl
from jax.experimental.pallas import tpu as pltpu
from jax.sharding import PartitionSpec as P

MESH = pl.DeviceIdType.MESH
TILE = 128
ROWS = 8
COLS = 16
GROUP = 384
HALF = 256
FAR = 5
OWN = 2
SLOTS = 6
ORDER = (OWN, 1, 3, 0, 4, FAR)
SOURCE = -1
RELAY = 5
ACROSS = 6
EVERY = frozenset(range(4))

ROUTES = (
    (-1, -1, -1, 0, 1, 0, -1, 21, 5, 3, 438, 60, 217, 41, 18, 194, 170, 138, 0),
    (-1, 1, -1, -1, 1, -1, -1, 289, 322, 220, 304, 295, 223, 246, 131, 165, 240, 149, 0),
    (-1, 1, -1, 4, 1, -1, -1, 288, 43, 406, 154, 118, 374, 232, 64, 220, 216, 81, 0),
    (17, 3, 5, 5, -1, 5, -1, 472, 457, 151, 313, 200, 56, 233, 97, 155, 107, 128, 20),
    (-1, -1, -1, -1, 2, -1, -1, 196, 18, 85, 299, 440, 26, 196, 50, 142, 236, 126, 0),
    (-1, -1, -1, 1, 0, -1, -1, 32, 306, 192, 319, 479, 237, 120, 112, 241, 234, 204, 0),
    (17, -1, 5, 5, 0, 0, -1, 16, 397, 214, 159, 2, 369, 52, 186, 214, 197, 227, 73),
    (7, -1, 3, 3, -1, 5, -1, 241, 386, 1, 137, 41, 64, 218, 239, 243, 180, 136, 26),
    (-1, 2, -1, -1, 2, 1, -1, 318, 250, 62, 112, 282, 403, 181, 151, 78, 201, 242, 0),
    (35, -1, 5, 5, 5, 5, -1, 401, 38, 328, 461, 274, 87, 21, 148, 133, 162, 150, 37),
    (-1, -1, -1, -1, 2, -1, -1, 358, 31, 183, 290, 127, 24, 159, 24, 130, 211, 62, 0),
    (-1, -1, -1, 1, -1, -1, -1, 293, 372, 197, 82, 80, 187, 103, 83, 173, 61, 15, 0),
    (-1, -1, -1, 0, 1, -1, -1, 207, 188, 25, 59, 149, 202, 23, 11, 210, 118, 14, 0),
    (-1, -1, -1, 1, 1, -1, -1, 102, 269, 364, 294, 199, 99, 4, 27, 116, 147, 48, 0),
    (-1, -1, -1, 4, 1, -1, -1, 86, 83, 257, 49, 420, 445, 8, 7, 183, 235, 28, 0),
    (-1, -1, -1, 4, 4, -1, -1, 271, 246, 194, 19, 71, 253, 33, 31, 100, 99, 3, 0),
    (35, -1, -1, 5, 4, -1, -1, 477, 352, 272, 76, 39, 266, 166, 176, 192, 217, 55, 91),
    (-1, -1, -1, 1, 0, -1, -1, 89, 162, 424, 28, 402, 210, 34, 47, 163, 169, 213, 0),
    (-1, -1, 4, 3, -1, -1, -1, 431, 362, 380, 6, 388, 171, 110, 247, 167, 42, 152, 0),
    (-1, -1, -1, 1, 0, -1, -1, 359, 191, 463, 446, 404, 130, 59, 89, 182, 206, 238, 0),
    (3, -1, -1, 0, -1, 5, -1, 165, 427, 176, 436, 42, 273, 36, 159, 208, 228, 185, 72),
    (-1, -1, -1, 1, 1, 1, -1, 270, 423, 175, 226, 116, 370, 119, 98, 203, 226, 189, 0),
    (44, -1, 5, 5, 4, -1, -1, 470, 321, 378, 320, 114, 139, 199, 222, 174, 177, 46, 75),
    (-1, -1, 4, 0, 4, -1, -1, 184, 218, 333, 145, 384, 235, 70, 224, 231, 212, 102, 0),
    (48, 5, -1, 5, -1, -1, -1, 344, 455, 74, 393, 327, 126, 171, 168, 178, 125, 93, 29),
    (-1, -1, -1, 3, -1, -1, -1, 92, 287, 133, 11, 169, 78, 17, 54, 104, 35, 39, 0),
    (-1, -1, 2, -1, 2, -1, -1, 260, 347, 224, 30, 382, 395, 49, 140, 44, 153, 68, 0),
    (-1, 1, -1, -1, 1, -1, -1, 166, 315, 351, 182, 256, 157, 157, 63, 106, 172, 22, 0),
    (-1, -1, -1, -1, 2, -1, -1, 468, 449, 476, 221, 70, 117, 58, 122, 108, 215, 59, 0),
    (-1, 2, -1, -1, 2, -1, -1, 168, 434, 0, 227, 466, 57, 114, 65, 38, 144, 101, 0),
    (-1, -1, -1, -1, 2, 0, -1, 350, 88, 280, 150, 456, 381, 96, 94, 85, 184, 229, 0),
    (-1, -1, -1, -1, 2, -1, -1, 452, 412, 408, 267, 433, 209, 146, 134, 139, 219, 90, 0),
    (-1, 1, -1, -1, -1, -1, -1, 4, 138, 447, 142, 426, 101, 145, 40, 0, 0, 0, 0),
    (-1, 1, -1, -1, -1, -1, -1, 95, 213, 232, 54, 123, 259, 193, 84, 0, 0, 0, 0),
    (-1, 1, -1, -1, -1, -1, -1, 249, 360, 238, 100, 55, 281, 0, 129, 0, 0, 0, 0),
    (-1, 1, -1, -1, -1, -1, -1, 285, 385, 409, 373, 262, 234, 0, 195, 0, 0, 0, 0),
    (-1, -1, -1, -1, -1, -1, -1, 469, 245, 153, 462, 65, 314, 175, 154, 0, 0, 0, 0),
    (-1, -1, 0, -1, -1, -1, -1, 375, 186, 212, 410, 411, 179, 123, 209, 0, 0, 0, 0),
    (4, 5, 5, -1, -1, -1, -1, 275, 185, 204, 105, 416, 233, 0, 221, 0, 0, 0, 115),
    (52, -1, 5, -1, -1, -1, -1, 301, 464, 181, 140, 8, 180, 0, 202, 0, 0, 0, 77),
    (12, 5, 5, -1, -1, -1, -1, 12, 144, 444, 276, 278, 297, 160, 205, 0, 0, 0, 86),
    (12, 5, 5, -1, -1, -1, -1, 219, 136, 195, 300, 361, 147, 69, 92, 0, 0, 0, 13),
    (-1, -1, -1, -1, -1, -1, -1, 465, 417, 251, 228, 104, 435, 0, 225, 0, 0, 0, 0),
    (-1, 1, -1, -1, -1, -1, -1, 242, 376, 239, 52, 132, 448, 0, 135, 0, 0, 0, 0),
    (-1, -1, 0, -1, -1, -1, -1, 310, 261, 173, 474, 336, 244, 0, 124, 0, 0, 0, 0),
    (4, -1, 5, -1, -1, -1, -1, 96, 216, 46, 170, 399, 243, 0, 132, 0, 0, 0, 25),
    (-1, -1, -1, -1, -1, -1, -1, 108, 205, 343, 467, 342, 383, 57, 105, 0, 0, 0, 0),
    (-1, -1, -1, -1, -1, -1, -1, 91, 109, 292, 164, 141, 79, 12, 53, 0, 0, 0, 0),
    (-1, 1, -1, -1, -1, -1, -1, 346, 35, 34, 247, 307, 429, 0, 19, 0, 0, 0, 0),
    (-1, 1, -1, -1, -1, -1, -1, 53, 340, 44, 279, 124, 330, 0, 45, 0, 0, 0, 0),
    (-1, -1, 0, -1, -1, -1, -1, 371, 451, 67, 428, 206, 120, 0, 6, 0, 0, 0, 0),
    (-1, 1, -1, -1, -1, -1, -1, 215, 10, 312, 400, 45, 143, 0, 1, 0, 0, 0, 0),
    (12, -1, 5, -1, -1, -1, -1, 113, 459, 33, 430, 121, 283, 0, 198, 0, 0, 0, 67),
    (4, -1, 5, -1, -1, -1, -1, 419, 236, 338, 189, 40, 324, 0, 111, 0, 0, 0, 16),
    (12, 5, 5, -1, -1, -1, -1, 354, 72, 255, 389, 134, 81, 141, 95, 0, 0, 0, 5),
    (-1, 1, -1, -1, -1, -1, -1, 337, 163, 335, 296, 268, 305, 74, 10, 0, 0, 0, 0),
    (57, 5, 5, -1, -1, -1, -1, 390, 291, 356, 379, 309, 316, 0, 237, 0, 0, 0, 127),
    (-1, -1, 0, -1, -1, -1, -1, 36, 367, 203, 363, 106, 13, 0, 187, 0, 0, 0, 0),
    (-1, 1, -1, -1, -1, -1, -1, 394, 190, 50, 58, 284, 355, 158, 56, 0, 0, 0, 0),
    (4, 5, 5, -1, -1, -1, -1, 61, 298, 29, 345, 17, 323, 143, 191, 0, 0, 0, 82),
    (-1, -1, -1, -1, -1, -1, -1, 94, 348, 172, 263, 413, 231, 0, 230, 0, 0, 0, 0),
    (-1, -1, 0, -1, -1, -1, -1, 471, 407, 27, 454, 473, 329, 0, 244, 0, 0, 0, 0),
    (-1, 1, -1, -1, -1, -1, -1, 158, 211, 339, 90, 225, 155, 245, 188, 0, 0, 0, 0),
    (-1, 1, -1, -1, -1, -1, -1, 334, 152, 240, 331, 332, 7, 200, 109, 0, 0, 0, 0),
    (-1, -1, 0, -1, -1, -1, -1, 37, 265, 14, 51, 422, 366, 0, 133, 0, 0, 0, 0),
    (-1, -1, -1, -1, -1, -1, -1, 148, 398, 110, 377, 73, 418, 0, 161, 0, 0, 0, 0),
    (-1, -1, -1, -1, -1, -1, -1, 432, 167, 405, 302, 15, 122, 156, 41, 0, 0, 0, 0),
    (-1, 1, -1, -1, -1, -1, -1, 47, 198, 115, 349, 161, 68, 190, 87, 0, 0, 0, 0),
    (-1, -1, 0, -1, -1, -1, -1, 421, 303, 392, 146, 443, 208, 9, 179, 0, 0, 0, 0),
    (12, 5, 5, -1, -1, -1, -1, 23, 326, 258, 387, 69, 450, 71, 66, 0, 0, 0, 2),
    (55, 5, -1, -1, -1, -1, -1, 177, 131, 201, 391, 475, 252, 0, 51, 0, 0, 0, 0),
    (-1, 1, -1, -1, -1, -1, -1, 353, 317, 396, 156, 478, 414, 0, 80, 0, 0, 0, 0),
    (-1, -1, -1, -1, -1, -1, -1, 439, 442, 222, 425, 248, 437, 79, 117, 0, 0, 0, 0),
    (-1, -1, -1, -1, -1, -1, -1, 308, 66, 77, 357, 75, 254, 32, 30, 0, 0, 0, 0),
    (-1, -1, -1, -1, -1, -1, -1, 48, 460, 22, 129, 160, 174, 76, 121, 0, 0, 0, 0),
    (-1, 1, -1, -1, -1, -1, -1, 368, 20, 63, 341, 97, 286, 113, 43, 0, 0, 0, 0),
    (-1, -1, -1, -1, -1, -1, -1, 441, 111, 98, 84, 365, 135, 223, 137, 0, 0, 0, 0),
    (-1, -1, -1, -1, -1, -1, -1, 93, 264, 325, 277, 229, 128, 60, 207, 0, 0, 0, 0),
    (-1, -1, -1, -1, -1, -1, -1, 9, 103, 453, 415, 107, 458, 0, 88, 0, 0, 0, 0),
    (-1, 1, -1, -1, -1, -1, -1, 193, 178, 119, 230, 125, 311, 0, 164, 0, 0, 0, 0),
)


def chip_of(device):
    return device[1] // 4, device[0] // 2, device[1] % 4


def role_of(device):
    x, y, z = chip_of(device)
    return (x - y) % 4, z, device[0] % 2


def p_kind(r, cp):
    m, h = cp // 2, cp % 2
    if m == r:
        return 0
    if (m == r + 1 and h == 0) or (m == r - 1 and h == 1):
        return 1
    return 2 if m == (r + 4) % ROWS else None


def p_pieces(kind, h):
    if kind == 0:
        return ((h, 0, 2, 0), (h, 2, 2, 1), (1 - h, 1 - h, 2, 2), (1 - h, 3 - h, 1, 3))
    half, start = (1 - h, h) if kind == 1 else (h, 0)
    return ((half, start, 2, 2), (half, start + 2, 1, 3))


def ap_pieces(slot):
    if slot == 4:
        return ((1, 2, 0), (3, 1, 1))
    return ((0, 2, 0), (2, 1 if slot in (0, FAR) else 2, 1))


def pieces():
    found = collections.OrderedDict()
    for r in range(ROWS):
        for cp in range(COLS):
            kind = p_kind(r, cp)
            if kind is None:
                continue
            z = cp % 4
            for n, (half, at, size, piece) in enumerate(p_pieces(kind, z % 2)):
                users = {n: (r, cp + d) for n, d in enumerate((-1, 1, -2, 2)) if 0 <= cp + d < COLS}
                users[4] = (r, (cp + 8) % COLS)
                entry = found.setdefault((0, kind, z, n), ((half, at, size, piece), []))
                entry[1].append(((r, cp), users))
    for r in range(ROWS):
        for c in range(COLS):
            for half in range(2):
                v = 2 * r + half - c
                slot = v + 2 if -2 <= v <= 2 else FAR if v in (8, -8) else None
                if slot is None:
                    continue
                x, y, z = chip_of((r, c))
                side = r - 1 + 2 * half
                for n, (at, size, piece) in enumerate(ap_pieces(slot)):
                    users = {1: ((r + 4) % ROWS, c)}
                    if 0 <= side < ROWS:
                        users[0 if side // 2 != r // 2 else ACROSS] = (side, c)
                    key = (1, r % 2, half, (x - y) % 4, z, n)
                    entry = found.setdefault(key, ((slot, half, at, size, piece), []))
                    entry[1].append(((r, c), users))
    return found


P_SLOT = (3, 1, 4, 0, FAR)

class Role:
    def __init__(self):
        self.sends = {}
        self.arrivals = {}
        self.greets = {}
        self.partners = {y: set() for y in range(4)}
        self.relayed = {}
        self.slabs = 0


def move_between(a, b):
    (ax, ay, _), (bx, by, bz) = chip_of(a), chip_of(b)
    return (bx - ax) % 4, (by - ay) % 4, bz, b[0] % 2


def make_plan():
    roles = {(a, z, core): Role() for a in range(4) for z in range(4) for core in range(2)}
    kinds = list(pieces().items())
    for n, (key, (_, instances)) in enumerate(kinds):
        size = kinds[n][1][0][3] if key[0] else kinds[n][1][0][2]
        offset, parents = ROUTES[n][0], ROUTES[n][1:7]
        for source, users in instances:
            place = dict(users)
            x, y, z = chip_of(source)
            if offset >= 0:
                rx, ry, rz = (x + offset % 4) % 4, (y + offset // 4 % 4) % 4, (z + offset // 16) % 4
                place[RELAY] = (2 * ry + source[0] % 2, 4 * rx + rz)
            place[SOURCE] = source
            reached = {SOURCE: SOURCE}
            edges = []

            def reach(node):
                if node in reached:
                    return reached[node]
                up = SOURCE if node == ACROSS else parents[node]
                if node not in place:
                    reached[node] = reach(up)
                    return reached[node]
                same = [u for u in users if node == RELAY and users[u] == place[RELAY]]
                if node == RELAY and place[RELAY] == source:
                    reached[node] = SOURCE
                    return SOURCE
                if same:
                    reached[same[0]] = same[0]
                    reached[node] = same[0]
                    edges.append((reach(up), same[0]))
                    return same[0]
                reached[node] = node
                edges.append((reach(up), node))
                return node

            if RELAY in place and RELAY in [parents[u] for u in users if u != ACROSS]:
                reach(RELAY)
            for user in users:
                reach(user)
            for a, b in edges:
                here, there = place[a], place[b]
                assert here != there
                mine, theirs = roles[role_of(here)], roles[role_of(there)]
                edge = (n, a, b, move_between(here, there))
                mine.sends.setdefault(edge, set()).add(here[0] // 2)
                theirs.arrivals.setdefault((n, b), set()).add(there[0] // 2)
                theirs.greets.setdefault(move_between(there, here), set()).add(there[0] // 2)
                mine.partners[here[0] // 2].add(there)
                if b == RELAY and n not in theirs.relayed:
                    theirs.relayed[n] = (theirs.slabs, len(theirs.relayed))
                    theirs.slabs += size
    return kinds, roles


KINDS, PLAN = make_plan()
MOST_SENDS = max(len(role.sends) for role in PLAN.values())
MOST_SLABS = max(max(role.slabs for role in PLAN.values()), 1)
MOST_RELAYED = max(max(len(role.relayed) for role in PLAN.values()), 1)


def target_role(role, move):
    return (role[0] + move[0] - move[1]) % 4, move[2], move[3]


def time_of(n, node):
    return -1 if node == ACROSS else ROUTES[n][13 + node]


def order_of_slots(role, member):
    latest = {slot: -1 for slot in ORDER}
    for (kind, node), members in PLAN[role].arrivals.items():
        if member in members and node != RELAY:
            key, (shape, _) = KINDS[kind]
            slot = shape[0] if key[0] else P_SLOT[node]
            latest[slot] = max(latest[slot], time_of(kind, node))
    return sum(slot * 8**n for n, slot in enumerate(sorted(ORDER, key=lambda slot: latest[slot])))


DIGITS = {(r, c): order_of_slots(role_of((r, c)), r // 2) for r in range(ROWS) for c in range(COLS)}


def column_of(c, slot):
    near = c + slot - 2
    far = slot == FAR
    cp = jnp.where(far, (c + 8) % COLS, near)
    return cp, far | ((near >= 0) & (near < COLS))


def shape_of(r, cp):
    m, h = cp // 2, cp % 2
    main = m == r
    low = (m == r + 1) & (h == 0)
    high = (m == r - 1) & (h == 1)
    far = m == (r + 4) % ROWS
    any3 = main | low | high | far
    half3 = jnp.where(far, h, 1 - h)
    start3 = jnp.where(main, 1 - h, jnp.where(high, 1, 0))
    return main, any3, half3, start3


def kernel(p_hbm, ap_hbm, pp_hbm, app_hbm, out_ref, pbuf, apbuf, relaybuf, pp_ref, app_ref,
           load_sem, send_sem, precv, aprecv, relayrecv):
    r = lax.axis_index("row")
    c = lax.axis_index("col")
    x, y, z, core = c // 4, r // 2, c % 4, r % 2
    diagonal = (x - y + 4) % 4
    is_y = [y == n for n in range(4)]

    def for_members(members, act):
        if members == EVERY:
            act()
        elif members:
            test = None
            for n in sorted(members):
                test = is_y[n] if test is None else test | is_y[n]
            pl.when(test)(act)

    def for_roles(act):
        def for_z(a):
            for zz in range(4):
                def for_core(zz=zz):
                    for cc in range(2):
                        pl.when(core == cc)(lambda cc=cc: act((a, zz, cc)))
                pl.when(z == zz)(for_core)
        for a in range(4):
            pl.when(diagonal == a)(lambda a=a: for_z(a))

    def device(move):
        return 2 * ((y + move[1]) % 4) + move[3], 4 * ((x + move[0]) % 4) + move[2]

    def region(n, node, role):
        key, (shape, _) = KINDS[n]
        if node == RELAY:
            first, index = PLAN[role].relayed[n]
            size = shape[3] if key[0] else shape[2]
            return relaybuf.at[pl.ds(first, size)], relayrecv.at[index]
        if key[0] == 0:
            half, at, size, piece = shape
            slot = OWN if node == SOURCE else P_SLOT[node]
            return pbuf.at[slot, half, pl.ds(at, size)], precv.at[slot, piece]
        slot, half, at, size, piece = shape
        return apbuf.at[half if node == SOURCE else 2 + slot, pl.ds(at, size)], aprecv.at[slot, piece]

    def copy_of(role, edge):
        n, a, b, move = edge
        source, _ = region(n, a, role)
        target, recv = region(n, b, target_role(role, move))
        return pltpu.make_async_remote_copy(
            src_ref=source,
            dst_ref=target,
            send_sem=send_sem.at[list(PLAN[role].sends).index(edge)],
            recv_sem=recv,
            device_id=device(move),
            device_id_type=MESH,
        )

    def arrived(role, n, node):
        target, recv = region(n, node, role)
        pltpu.make_async_remote_copy(
            src_ref=target, dst_ref=target, send_sem=send_sem.at[0], recv_sem=recv,
            device_id=(r, c), device_id_type=MESH,
        ).wait_recv()

    def order_of(edge):
        n, _, b, _ = edge
        return -1 if b == ACROSS else ROUTES[n][7 + b]

    def passed_on(role):
        found = {}
        for (n, a, _, _), members in PLAN[role].sends.items():
            if a != SOURCE:
                found.setdefault((n, a), set()).update(members)
        return found

    barrier = pltpu.get_barrier_semaphore()

    def greet(role):
        for move, members in sorted(PLAN[role].greets.items()):
            for_members(members, lambda move=move: pl.semaphore_signal(
                barrier, inc=1, device_id=device(move), device_id_type=MESH))

    def send(role):
        plan = PLAN[role]
        counts = {}
        for n, partners in plan.partners.items():
            counts.setdefault(len(partners), set()).add(n)
        for count, members in counts.items():
            if count:
                for_members(members, lambda count=count: pl.semaphore_wait(barrier, count))
        for edge in sorted((e for e in plan.sends if e[1] == SOURCE), key=order_of):
            for_members(plan.sends[edge], lambda edge=edge: copy_of(role, edge).start())
        waits = sorted(passed_on(role).items(), key=lambda item: time_of(*item[0]))
        for (n, node), members in waits:
            for_members(members, lambda n=n, node=node: arrived(role, n, node))
            for edge in sorted((e for e in plan.sends if e[:2] == (n, node)), key=order_of):
                for_members(plan.sends[edge], lambda edge=edge: copy_of(role, edge).start())

    def finish(role):
        for edge, members in PLAN[role].sends.items():
            for_members(members, lambda edge=edge: copy_of(role, edge).wait_send())

    def await_step(step):
        def one(role):
            handed = passed_on(role)
            by_step = {}
            for (n, node), members in PLAN[role].arrivals.items():
                left = members - handed.get((n, node), set())
                if node == RELAY or not left:
                    continue
                key, (shape, _) = KINDS[n]
                at = 2 * shape[0] if key[0] else 2 * P_SLOT[node] + shape[0]
                by_step.setdefault(at, []).append((n, node, left))
            for at, waits in sorted(by_step.items()):
                @pl.when(step == at)
                def _():
                    for n, node, left in waits:
                        for_members(left, lambda n=n, node=node: arrived(role, n, node))

        for_roles(one)

    for_roles(greet)

    loads = []
    for g in range(2):
        for i in range(4):
            loads.append(pltpu.make_async_copy(
                p_hbm.at[pl.ds(g * GROUP, GROUP), pl.ds(i * TILE, TILE)],
                pbuf.at[OWN, i // 2, 2 * g + 1 - i % 2],
                load_sem.at[4 * g + i],
            ))
    for q in range(4):
        for j in range(2):
            loads.append(pltpu.make_async_copy(
                ap_hbm.at[pl.ds(q * GROUP, GROUP), pl.ds(j * TILE, TILE)],
                apbuf.at[q // 2, 2 * j + 1 - q % 2],
                load_sem.at[8 + 2 * q + j],
            ))
    loads.append(pltpu.make_async_copy(pp_hbm, pp_ref, load_sem.at[16]))
    loads.append(pltpu.make_async_copy(app_hbm, app_ref, load_sem.at[17]))
    for load in loads:
        load.start()
    for load in loads:
        load.wait()
    for a in range(6):
        g, rows = a // 3, pl.ds(a % 3 * TILE, TILE)
        for i in range(4):
            weight = pp_ref[i, a].astype(jnp.float32).astype(jnp.bfloat16)
            slab = (OWN, i // 2, 2 * g + 1 - i % 2, rows)
            pbuf[slab] = pbuf[slab] * weight
    for a in range(12):
        q, rows = a // 3, pl.ds(a % 3 * TILE, TILE)
        for j in range(2):
            weight = app_ref[j, a].astype(jnp.float32).astype(jnp.bfloat16)
            slab = (q // 2, 2 * j + 1 - q % 2, rows)
            apbuf[slab] = apbuf[slab] * weight

    for_roles(send)

    blank = jnp.zeros((GROUP, TILE), jnp.bfloat16)
    apbuf[2 + 0, 3] = blank
    apbuf[2 + 4, 0] = blank
    apbuf[2 + FAR, 3] = blank
    for slot in range(SLOTS):
        if slot != OWN:
            cp, ok = column_of(c, slot)
            _, any3, half, start = shape_of(r, cp)

            @pl.when(ok & any3)
            def _():
                pbuf[slot, half, jnp.where(start == 0, 3, 0)] = blank
    out_ref[...] = jnp.zeros_like(out_ref)

    number = r * COLS + c
    usual = collections.Counter(DIGITS.values()).most_common(1)[0][0]
    digits = jnp.int32(usual)
    for (row, col), order in DIGITS.items():
        if order != usual:
            digits = jnp.where(number == row * COLS + col, order, digits)

    def multiply(step, digits):
        t = step % 2
        slot = digits % 8
        cp, ok = column_of(c, slot)
        main, any3, half3, _ = shape_of(r, cp)
        m, h = cp // 2, cp % 2
        full = main & (t == h)
        part = any3 & (t == half3)
        await_step(2 * slot + t)

        @pl.when(ok & (full | part))
        def _():
            ap_index = jnp.where(m == r, h, 2 + slot)
            rows = pl.ds(pl.multiple_of(t * HALF, HALF), HALF)
            left = jnp.concatenate([
                jnp.concatenate([pbuf[slot, t, 2 * g + 1], pbuf[slot, t, 2 * g]], axis=1) for g in range(2)
            ], axis=0)
            right = jnp.concatenate([
                jnp.concatenate([apbuf[ap_index, 1 - g], apbuf[ap_index, 3 - g]], axis=1) for g in range(2)
            ], axis=0)
            out_ref[rows, :] += lax.dot_general(
                left, right, (((0,), (0,)), ((), ())), preferred_element_type=jnp.float32
            )

        return jnp.where(t == 1, digits // 8, digits)

    lax.fori_loop(0, 2 * SLOTS, multiply, digits)
    for_roles(finish)


def on_device(prolong, applied, prolong_pattern, applied_pattern):
    return pl.pallas_call(
        kernel,
        out_shape=jax.ShapeDtypeStruct((prolong.shape[1], applied.shape[1]), jnp.float32),
        in_specs=[
            pl.BlockSpec(memory_space=pl.ANY),
            pl.BlockSpec(memory_space=pl.ANY),
            pl.BlockSpec(memory_space=pl.ANY),
            pl.BlockSpec(memory_space=pl.ANY),
        ],
        out_specs=pl.BlockSpec(memory_space=pltpu.VMEM),
        scratch_shapes=[
            pltpu.VMEM((SLOTS, 2, 4, GROUP, TILE), jnp.bfloat16),
            pltpu.VMEM((2 + SLOTS, 4, GROUP, TILE), jnp.bfloat16),
            pltpu.VMEM((MOST_SLABS, GROUP, TILE), jnp.bfloat16),
            pltpu.SMEM((4, 6), jnp.int32),
            pltpu.SMEM((2, 12), jnp.int32),
            pltpu.SemaphoreType.DMA((18,)),
            pltpu.SemaphoreType.DMA((MOST_SENDS,)),
            pltpu.SemaphoreType.DMA((SLOTS, 4)),
            pltpu.SemaphoreType.DMA((SLOTS, 2)),
            pltpu.SemaphoreType.DMA((MOST_RELAYED,)),
        ],
        compiler_params=pltpu.CompilerParams(
            collective_id=0, has_side_effects=True, vmem_limit_bytes=56000000
        ),
    )(
        prolong,
        applied,
        pltpu.with_memory_space_constraint(prolong_pattern.T, pltpu.HBM),
        pltpu.with_memory_space_constraint(applied_pattern.T, pltpu.HBM),
    )


def solution(mesh):
    in_specs = (P("col", "row"), P("row", "col"), P("col", "row"), P("row", "col"))
    out_specs = P("row", "col")
    return jax.shard_map(
        on_device, mesh=mesh, in_specs=in_specs, out_specs=out_specs, check_vma=False
    )
```

```python
import collections

import jax
import jax.numpy as jnp
from jax import lax
from jax.experimental import pallas as pl
from jax.experimental.pallas import tpu as pltpu
from jax.sharding import PartitionSpec as P

MESH = pl.DeviceIdType.MESH
TILE = 128
ROWS = 8
COLS = 16
GROUP = 384
HALF = 256
FAR = 5
OWN = 2
SLOTS = 6
ORDER = (OWN, 1, 3, 0, 4, FAR)
SOURCE = -1
RELAY = 5
ACROSS = 6
EVERY = frozenset(range(4))

ROUTES = (
    (-1, -1, -1, 0, 1, 0, -1, 62, 87, 337, 250, 54, 229, 42, 19, 180, 176, 166, 0),
    (-1, 1, -1, -1, 1, -1, -1, 412, 396, 367, 103, 329, 21, 245, 74, 154, 230, 162, 0),
    (-1, 1, -1, 4, 1, -1, -1, 255, 406, 307, 281, 163, 335, 261, 114, 231, 254, 62, 0),
    (17, 3, 5, 5, -1, 5, -1, 277, 290, 262, 298, 429, 239, 259, 143, 181, 173, 184, 56),
    (-1, -1, -1, -1, 2, -1, -1, 383, 106, 76, 427, 293, 265, 200, 64, 121, 235, 133, 0),
    (-1, -1, -1, 1, 0, -1, -1, 333, 404, 74, 270, 476, 321, 132, 107, 253, 236, 194, 0),
    (17, -1, 5, 5, 0, 0, -1, 279, 238, 205, 124, 414, 17, 84, 198, 234, 182, 241, 72),
    (19, 3, 5, 5, -1, 5, -1, 154, 269, 351, 157, 343, 16, 155, 147, 118, 37, 152, 30),
    (-1, 2, -1, -1, 2, 1, -1, 49, 374, 33, 446, 449, 219, 213, 159, 85, 219, 258, 0),
    (35, -1, 0, 5, 5, 5, -1, 46, 461, 240, 110, 86, 313, 33, 251, 188, 167, 221, 69),
    (-1, -1, -1, 3, -1, -1, -1, 439, 252, 31, 381, 132, 257, 100, 106, 218, 77, 49, 0),
    (-1, -1, -1, 0, 1, -1, -1, 320, 417, 183, 166, 369, 319, 127, 52, 237, 185, 103, 54),
    (-1, -1, -1, -1, 2, -1, -1, 148, 139, 44, 310, 273, 349, 80, 43, 170, 212, 68, 0),
    (-1, -1, -1, -1, 1, -1, -1, 466, 150, 182, 430, 51, 13, 11, 156, 144, 38, 17, 14),
    (-1, -1, -1, 4, 1, -1, -1, 175, 99, 71, 5, 81, 249, 4, 8, 157, 248, 9, 0),
    (-1, 4, -1, 4, 4, -1, -1, 212, 428, 82, 340, 263, 121, 21, 34, 204, 256, 31, 0),
    (35, -1, -1, 5, 5, -1, -1, 401, 388, 198, 228, 409, 189, 250, 197, 193, 226, 110, 78),
    (-1, -1, -1, 1, 0, -1, -1, 116, 96, 370, 128, 377, 211, 47, 88, 186, 232, 220, 0),
    (-1, -1, 4, 3, -1, -1, -1, 216, 41, 57, 18, 305, 186, 150, 262, 148, 41, 171, 0),
    (-1, -1, -1, 1, 0, -1, -1, 256, 194, 64, 447, 443, 193, 93, 134, 206, 187, 243, 0),
    (3, -1, 5, 0, -1, 5, -1, 236, 12, 363, 469, 168, 248, 86, 214, 203, 172, 223, 61),
    (-1, -1, -1, 1, 1, 1, -1, 356, 387, 197, 20, 174, 1, 246, 104, 233, 209, 217, 0),
    (44, -1, -1, 5, 5, -1, -1, 380, 448, 83, 454, 415, 14, 158, 242, 190, 222, 137, 95),
    (-1, -1, 4, 0, 4, -1, -1, 312, 42, 271, 259, 84, 467, 207, 161, 66, 142, 36, 0),
    (-1, -1, -1, 0, 1, -1, -1, 67, 287, 231, 336, 140, 306, 97, 65, 249, 164, 102, 48),
    (-1, -1, -1, 0, 1, 1, -1, 38, 35, 180, 474, 111, 215, 23, 12, 255, 191, 119, 0),
    (-1, -1, 2, -1, 2, -1, -1, 223, 258, 460, 456, 191, 230, 115, 224, 76, 202, 75, 0),
    (5, 5, -1, 1, 5, -1, -1, 0, 53, 368, 384, 338, 70, 22, 13, 124, 149, 20, 0),
    (-1, -1, 4, -1, 0, -1, -1, 37, 201, 435, 472, 90, 178, 105, 153, 98, 215, 99, 0),
    (53, -1, -1, 0, 5, -1, -1, 288, 437, 272, 346, 458, 420, 139, 91, 141, 184, 32, 0),
    (-1, -1, -1, -1, 2, 0, -1, 142, 24, 28, 123, 105, 324, 125, 140, 94, 189, 247, 0),
    (-1, -1, -1, -1, 2, -1, -1, 296, 190, 379, 113, 275, 426, 79, 57, 238, 174, 101, 87),
    (4, -1, 5, -1, -1, -1, -1, 403, 131, 204, 372, 91, 210, 113, 179, 0, 0, 0, 70),
    (-1, -1, 0, -1, -1, -1, -1, 29, 391, 26, 172, 241, 267, 35, 160, 0, 0, 0, 0),
    (-1, 1, -1, -1, -1, -1, -1, 151, 375, 438, 39, 89, 433, 0, 163, 0, 0, 0, 0),
    (-1, -1, -1, -1, -1, -1, -1, 425, 134, 444, 209, 303, 177, 0, 71, 0, 0, 0, 0),
    (-1, -1, 0, -1, -1, -1, -1, 170, 100, 95, 261, 398, 10, 122, 244, 0, 0, 0, 0),
    (-1, -1, -1, -1, -1, -1, -1, 328, 192, 72, 422, 65, 108, 201, 192, 0, 0, 0, 0),
    (4, -1, 5, -1, -1, -1, -1, 200, 459, 55, 418, 237, 184, 0, 227, 0, 0, 0, 120),
    (-1, 1, -1, -1, -1, -1, -1, 331, 138, 135, 79, 118, 69, 0, 92, 0, 0, 0, 108),
    (12, 5, 5, -1, -1, -1, -1, 441, 300, 278, 440, 78, 207, 126, 178, 0, 0, 0, 53),
    (-1, -1, 0, -1, -1, -1, -1, 220, 243, 264, 45, 232, 11, 168, 205, 0, 0, 0, 16),
    (4, 5, 5, -1, -1, -1, -1, 27, 30, 22, 233, 188, 468, 0, 240, 0, 0, 0, 138),
    (-1, -1, 0, -1, -1, -1, -1, 208, 341, 359, 311, 390, 187, 0, 151, 0, 0, 0, 0),
    (-1, 1, -1, -1, -1, -1, -1, 68, 34, 136, 88, 242, 251, 0, 146, 0, 0, 0, 0),
    (-1, -1, -1, -1, -1, -1, -1, 143, 164, 413, 297, 173, 318, 0, 46, 0, 0, 0, 26),
    (-1, -1, -1, -1, -1, -1, -1, 247, 402, 445, 43, 176, 147, 96, 50, 0, 0, 0, 0),
    (-1, -1, 0, -1, -1, -1, -1, 365, 214, 221, 126, 350, 2, 128, 90, 0, 0, 0, 27),
    (-1, 1, -1, -1, -1, -1, -1, 19, 334, 92, 246, 202, 268, 0, 58, 0, 0, 0, 0),
    (-1, 1, -1, -1, -1, -1, -1, 376, 50, 419, 6, 282, 342, 0, 89, 0, 0, 0, 15),
    (-1, -1, 0, -1, -1, -1, -1, 327, 477, 436, 167, 66, 161, 0, 7, 0, 0, 0, 0),
    (-1, -1, 0, -1, -1, -1, -1, 226, 475, 385, 59, 473, 455, 0, 2, 0, 0, 0, 1),
    (12, 5, 5, -1, -1, -1, -1, 120, 353, 348, 355, 463, 274, 0, 196, 0, 0, 0, 67),
    (4, 5, 5, -1, -1, -1, -1, 141, 332, 107, 308, 291, 283, 0, 145, 0, 0, 0, 28),
    (12, 5, 5, -1, -1, -1, -1, 285, 366, 181, 152, 245, 179, 116, 129, 0, 0, 0, 5),
    (4, 5, 5, -1, -1, -1, -1, 3, 23, 109, 80, 295, 63, 10, 44, 0, 0, 0, 3),
    (57, 5, 5, -1, -1, -1, -1, 117, 206, 149, 462, 345, 304, 0, 252, 0, 0, 0, 136),
    (-1, -1, 0, -1, -1, -1, -1, 130, 235, 7, 326, 434, 125, 0, 117, 0, 0, 0, 0),
    (-1, -1, -1, -1, -1, -1, -1, 471, 330, 48, 452, 155, 389, 229, 208, 0, 0, 0, 0),
    (4, 5, 5, -1, -1, -1, -1, 85, 129, 225, 254, 93, 32, 101, 165, 0, 0, 0, 39),
    (-1, 1, -1, -1, -1, -1, -1, 280, 442, 61, 289, 411, 4, 0, 239, 0, 0, 0, 0),
    (-1, -1, 0, -1, -1, -1, -1, 386, 354, 25, 314, 465, 371, 0, 260, 0, 0, 0, 0),
    (-1, 1, -1, -1, -1, -1, -1, 407, 165, 451, 292, 160, 464, 257, 195, 0, 0, 0, 0),
    (-1, 1, -1, -1, -1, -1, -1, 410, 156, 315, 260, 316, 185, 225, 135, 0, 0, 0, 0),
    (12, -1, 5, -1, -1, -1, -1, 276, 227, 114, 104, 234, 94, 0, 112, 0, 0, 0, 60),
    (-1, -1, -1, -1, -1, -1, -1, 431, 399, 115, 58, 299, 137, 0, 29, 0, 0, 0, 0),
    (-1, -1, -1, -1, -1, -1, -1, 360, 325, 364, 97, 394, 378, 216, 169, 0, 0, 0, 63),
    (-1, -1, 0, -1, -1, -1, -1, 301, 195, 421, 47, 145, 77, 55, 210, 0, 0, 0, 0),
    (-1, -1, 0, -1, -1, -1, -1, 101, 323, 199, 36, 362, 309, 6, 175, 0, 0, 0, 0),
    (-1, 1, -1, -1, -1, -1, -1, 479, 75, 266, 52, 196, 286, 131, 25, 0, 0, 0, 59),
    (-1, 1, -1, -1, -1, -1, -1, 457, 218, 60, 395, 358, 432, 0, 51, 0, 0, 0, 0),
    (-1, 1, -1, -1, -1, -1, -1, 153, 8, 382, 144, 478, 244, 0, 81, 0, 0, 0, 0),
    (-1, -1, -1, -1, -1, -1, -1, 112, 470, 322, 159, 294, 302, 40, 111, 0, 0, 0, 0),
    (-1, -1, 0, -1, -1, -1, -1, 416, 224, 217, 213, 127, 146, 73, 123, 0, 0, 0, 18),
    (-1, -1, -1, -1, -1, -1, -1, 339, 453, 397, 361, 222, 317, 211, 109, 0, 0, 0, 24),
    (-1, -1, 0, -1, -1, -1, -1, 9, 73, 171, 344, 56, 98, 83, 45, 0, 0, 0, 0),
    (-1, 1, -1, -1, -1, -1, -1, 162, 102, 253, 400, 169, 133, 228, 82, 0, 0, 0, 0),
    (-1, -1, -1, -1, -1, -1, -1, 284, 405, 450, 40, 424, 203, 183, 177, 0, 0, 0, 0),
    (-1, -1, 0, -1, -1, -1, -1, 158, 122, 408, 357, 119, 423, 0, 130, 0, 0, 0, 0),
    (-1, -1, -1, -1, -1, -1, -1, 393, 347, 392, 15, 352, 373, 0, 199, 0, 0, 0, 0),
)


def chip_of(device):
    return device[1] // 4, device[0] // 2, device[1] % 4


def role_of(device):
    x, y, z = chip_of(device)
    return (x - y) % 4, z, device[0] % 2


def p_kind(r, cp):
    m, h = cp // 2, cp % 2
    if m == r:
        return 0
    if (m == r + 1 and h == 0) or (m == r - 1 and h == 1):
        return 1
    return 2 if m == (r + 4) % ROWS else None


def p_pieces(kind, h):
    if kind == 0:
        return ((h, 0, 2, 0), (h, 2, 2, 1), (1 - h, 1 - h, 2, 2), (1 - h, 3 - h, 1, 3))
    half, start = (1 - h, h) if kind == 1 else (h, 0)
    return ((half, start, 2, 2), (half, start + 2, 1, 3))


def ap_pieces(slot):
    if slot == 4:
        return ((1, 2, 0), (3, 1, 1))
    return ((0, 2, 0), (2, 1 if slot in (0, FAR) else 2, 1))


def pieces():
    found = collections.OrderedDict()
    for r in range(ROWS):
        for cp in range(COLS):
            kind = p_kind(r, cp)
            if kind is None:
                continue
            z = cp % 4
            for n, (half, at, size, piece) in enumerate(p_pieces(kind, z % 2)):
                users = {n: (r, cp + d) for n, d in enumerate((-1, 1, -2, 2)) if 0 <= cp + d < COLS}
                users[4] = (r, (cp + 8) % COLS)
                entry = found.setdefault((0, kind, z, n), ((half, at, size, piece), []))
                entry[1].append(((r, cp), users))
    for r in range(ROWS):
        for c in range(COLS):
            for half in range(2):
                v = 2 * r + half - c
                slot = v + 2 if -2 <= v <= 2 else FAR if v in (8, -8) else None
                if slot is None:
                    continue
                x, y, z = chip_of((r, c))
                side = r - 1 + 2 * half
                for n, (at, size, piece) in enumerate(ap_pieces(slot)):
                    users = {1: ((r + 4) % ROWS, c)}
                    if 0 <= side < ROWS:
                        users[0 if side // 2 != r // 2 else ACROSS] = (side, c)
                    key = (1, r % 2, half, (x - y) % 4, z, n)
                    entry = found.setdefault(key, ((slot, half, at, size, piece), []))
                    entry[1].append(((r, c), users))
    return found


P_SLOT = (3, 1, 4, 0, FAR)

class Role:
    def __init__(self):
        self.sends = {}
        self.arrivals = {}
        self.greets = {}
        self.partners = {y: set() for y in range(4)}
        self.relayed = {}
        self.slabs = 0


def move_between(a, b):
    (ax, ay, _), (bx, by, bz) = chip_of(a), chip_of(b)
    return (bx - ax) % 4, (by - ay) % 4, bz, b[0] % 2


def make_plan():
    roles = {(a, z, core): Role() for a in range(4) for z in range(4) for core in range(2)}
    kinds = list(pieces().items())
    for n, (key, (_, instances)) in enumerate(kinds):
        size = kinds[n][1][0][3] if key[0] else kinds[n][1][0][2]
        offset, parents = ROUTES[n][0], ROUTES[n][1:7]
        for source, users in instances:
            place = dict(users)
            x, y, z = chip_of(source)
            if offset >= 0:
                rx, ry, rz = (x + offset % 4) % 4, (y + offset // 4 % 4) % 4, (z + offset // 16) % 4
                place[RELAY] = (2 * ry + source[0] % 2, 4 * rx + rz)
            place[SOURCE] = source
            reached = {SOURCE: SOURCE}
            edges = []

            def reach(node):
                if node in reached:
                    return reached[node]
                up = SOURCE if node == ACROSS else parents[node]
                if node not in place:
                    reached[node] = reach(up)
                    return reached[node]
                same = [u for u in users if node == RELAY and users[u] == place[RELAY]]
                if node == RELAY and place[RELAY] == source:
                    reached[node] = SOURCE
                    return SOURCE
                if same:
                    reached[same[0]] = same[0]
                    reached[node] = same[0]
                    edges.append((reach(up), same[0]))
                    return same[0]
                reached[node] = node
                edges.append((reach(up), node))
                return node

            if RELAY in place and RELAY in [parents[u] for u in users if u != ACROSS]:
                reach(RELAY)
            for user in users:
                reach(user)
            for a, b in edges:
                here, there = place[a], place[b]
                assert here != there
                mine, theirs = roles[role_of(here)], roles[role_of(there)]
                edge = (n, a, b, move_between(here, there))
                mine.sends.setdefault(edge, set()).add(here[0] // 2)
                theirs.arrivals.setdefault((n, b), set()).add(there[0] // 2)
                theirs.greets.setdefault(move_between(there, here), set()).add(there[0] // 2)
                mine.partners[here[0] // 2].add(there)
                if b == RELAY and n not in theirs.relayed:
                    theirs.relayed[n] = (theirs.slabs, len(theirs.relayed))
                    theirs.slabs += size
    return kinds, roles


KINDS, PLAN = make_plan()
MOST_SENDS = max(len(role.sends) for role in PLAN.values())
MOST_SLABS = max(max(role.slabs for role in PLAN.values()), 1)
MOST_RELAYED = max(max(len(role.relayed) for role in PLAN.values()), 1)


def target_role(role, move):
    return (role[0] + move[0] - move[1]) % 4, move[2], move[3]


def time_of(n, node):
    return -1 if node == ACROSS else ROUTES[n][13 + node]


def order_of_slots(role, member):
    latest = {slot: -1 for slot in ORDER}
    for (kind, node), members in PLAN[role].arrivals.items():
        if member in members and node != RELAY:
            key, (shape, _) = KINDS[kind]
            slot = shape[0] if key[0] else P_SLOT[node]
            latest[slot] = max(latest[slot], time_of(kind, node))
    return sum(slot * 8**n for n, slot in enumerate(sorted(ORDER, key=lambda slot: latest[slot])))


DIGITS = {(r, c): order_of_slots(role_of((r, c)), r // 2) for r in range(ROWS) for c in range(COLS)}


def column_of(c, slot):
    near = c + slot - 2
    far = slot == FAR
    cp = jnp.where(far, (c + 8) % COLS, near)
    return cp, far | ((near >= 0) & (near < COLS))


def shape_of(r, cp):
    m, h = cp // 2, cp % 2
    main = m == r
    low = (m == r + 1) & (h == 0)
    high = (m == r - 1) & (h == 1)
    far = m == (r + 4) % ROWS
    any3 = main | low | high | far
    half3 = jnp.where(far, h, 1 - h)
    start3 = jnp.where(main, 1 - h, jnp.where(high, 1, 0))
    return main, any3, half3, start3


def kernel(p_hbm, ap_hbm, pp_hbm, app_hbm, out_ref, pbuf, apbuf, relaybuf, pp_ref, app_ref,
           load_sem, send_sem, precv, aprecv, relayrecv):
    r = lax.axis_index("row")
    c = lax.axis_index("col")
    x, y, z, core = c // 4, r // 2, c % 4, r % 2
    diagonal = (x - y + 4) % 4
    is_y = [y == n for n in range(4)]

    def for_members(members, act):
        if members == EVERY:
            act()
        elif members:
            test = None
            for n in sorted(members):
                test = is_y[n] if test is None else test | is_y[n]
            pl.when(test)(act)

    def for_roles(act):
        def for_z(a):
            for zz in range(4):
                def for_core(zz=zz):
                    for cc in range(2):
                        pl.when(core == cc)(lambda cc=cc: act((a, zz, cc)))
                pl.when(z == zz)(for_core)
        for a in range(4):
            pl.when(diagonal == a)(lambda a=a: for_z(a))

    def device(move):
        return 2 * ((y + move[1]) % 4) + move[3], 4 * ((x + move[0]) % 4) + move[2]

    def region(n, node, role):
        key, (shape, _) = KINDS[n]
        if node == RELAY:
            first, index = PLAN[role].relayed[n]
            size = shape[3] if key[0] else shape[2]
            return relaybuf.at[pl.ds(first, size)], relayrecv.at[index]
        if key[0] == 0:
            half, at, size, piece = shape
            slot = OWN if node == SOURCE else P_SLOT[node]
            return pbuf.at[slot, half, pl.ds(at, size)], precv.at[slot, piece]
        slot, half, at, size, piece = shape
        return apbuf.at[half if node == SOURCE else 2 + slot, pl.ds(at, size)], aprecv.at[slot, piece]

    def copy_of(role, edge):
        n, a, b, move = edge
        source, _ = region(n, a, role)
        target, recv = region(n, b, target_role(role, move))
        return pltpu.make_async_remote_copy(
            src_ref=source,
            dst_ref=target,
            send_sem=send_sem.at[list(PLAN[role].sends).index(edge)],
            recv_sem=recv,
            device_id=device(move),
            device_id_type=MESH,
        )

    def arrived(role, n, node):
        target, recv = region(n, node, role)
        pltpu.make_async_remote_copy(
            src_ref=target, dst_ref=target, send_sem=send_sem.at[0], recv_sem=recv,
            device_id=(r, c), device_id_type=MESH,
        ).wait_recv()

    def order_of(edge):
        n, _, b, _ = edge
        return -1 if b == ACROSS else ROUTES[n][7 + b]

    def passed_on(role):
        found = {}
        for (n, a, _, _), members in PLAN[role].sends.items():
            if a != SOURCE:
                found.setdefault((n, a), set()).update(members)
        return found

    barrier = pltpu.get_barrier_semaphore()

    def greet(role):
        for move, members in sorted(PLAN[role].greets.items()):
            for_members(members, lambda move=move: pl.semaphore_signal(
                barrier, inc=1, device_id=device(move), device_id_type=MESH))

    def send(role):
        plan = PLAN[role]
        counts = {}
        for n, partners in plan.partners.items():
            counts.setdefault(len(partners), set()).add(n)
        for count, members in counts.items():
            if count:
                for_members(members, lambda count=count: pl.semaphore_wait(barrier, count))
        for edge in sorted((e for e in plan.sends if e[1] == SOURCE), key=order_of):
            for_members(plan.sends[edge], lambda edge=edge: copy_of(role, edge).start())
        waits = sorted(passed_on(role).items(), key=lambda item: time_of(*item[0]))
        for (n, node), members in waits:
            for_members(members, lambda n=n, node=node: arrived(role, n, node))
            for edge in sorted((e for e in plan.sends if e[:2] == (n, node)), key=order_of):
                for_members(plan.sends[edge], lambda edge=edge: copy_of(role, edge).start())

    def finish(role):
        for edge, members in PLAN[role].sends.items():
            for_members(members, lambda edge=edge: copy_of(role, edge).wait_send())

    def await_step(step):
        def one(role):
            handed = passed_on(role)
            by_step = {}
            for (n, node), members in PLAN[role].arrivals.items():
                left = members - handed.get((n, node), set())
                if node == RELAY or not left:
                    continue
                key, (shape, _) = KINDS[n]
                at = 2 * shape[0] if key[0] else 2 * P_SLOT[node] + shape[0]
                by_step.setdefault(at, []).append((n, node, left))
            for at, waits in sorted(by_step.items()):
                @pl.when(step == at)
                def _():
                    for n, node, left in waits:
                        for_members(left, lambda n=n, node=node: arrived(role, n, node))

        for_roles(one)

    for_roles(greet)

    loads = []
    for g in range(2):
        for i in range(4):
            loads.append(pltpu.make_async_copy(
                p_hbm.at[pl.ds(g * GROUP, GROUP), pl.ds(i * TILE, TILE)],
                pbuf.at[OWN, i // 2, 2 * g + 1 - i % 2],
                load_sem.at[4 * g + i],
            ))
    for q in range(4):
        for j in range(2):
            loads.append(pltpu.make_async_copy(
                ap_hbm.at[pl.ds(q * GROUP, GROUP), pl.ds(j * TILE, TILE)],
                apbuf.at[q // 2, 2 * j + 1 - q % 2],
                load_sem.at[8 + 2 * q + j],
            ))
    loads.append(pltpu.make_async_copy(pp_hbm, pp_ref, load_sem.at[16]))
    loads.append(pltpu.make_async_copy(app_hbm, app_ref, load_sem.at[17]))
    for load in loads:
        load.start()
    for load in loads:
        load.wait()
    for a in range(6):
        g, rows = a // 3, pl.ds(a % 3 * TILE, TILE)
        for i in range(4):
            weight = pp_ref[i, a].astype(jnp.float32).astype(jnp.bfloat16)
            slab = (OWN, i // 2, 2 * g + 1 - i % 2, rows)
            pbuf[slab] = pbuf[slab] * weight
    for a in range(12):
        q, rows = a // 3, pl.ds(a % 3 * TILE, TILE)
        for j in range(2):
            weight = app_ref[j, a].astype(jnp.float32).astype(jnp.bfloat16)
            slab = (q // 2, 2 * j + 1 - q % 2, rows)
            apbuf[slab] = apbuf[slab] * weight

    for_roles(send)

    blank = jnp.zeros((GROUP, TILE), jnp.bfloat16)
    apbuf[2 + 0, 3] = blank
    apbuf[2 + 4, 0] = blank
    apbuf[2 + FAR, 3] = blank
    for slot in range(SLOTS):
        if slot != OWN:
            cp, ok = column_of(c, slot)
            _, any3, half, start = shape_of(r, cp)

            @pl.when(ok & any3)
            def _():
                pbuf[slot, half, jnp.where(start == 0, 3, 0)] = blank
    out_ref[...] = jnp.zeros_like(out_ref)

    number = r * COLS + c
    usual = collections.Counter(DIGITS.values()).most_common(1)[0][0]
    digits = jnp.int32(usual)
    for (row, col), order in DIGITS.items():
        if order != usual:
            digits = jnp.where(number == row * COLS + col, order, digits)

    def multiply(step, digits):
        t = step % 2
        slot = digits % 8
        cp, ok = column_of(c, slot)
        main, any3, half3, _ = shape_of(r, cp)
        m, h = cp // 2, cp % 2
        full = main & (t == h)
        part = any3 & (t == half3)
        await_step(2 * slot + t)

        @pl.when(ok & (full | part))
        def _():
            ap_index = jnp.where(m == r, h, 2 + slot)
            rows = pl.ds(pl.multiple_of(t * HALF, HALF), HALF)
            left = jnp.concatenate([
                jnp.concatenate([pbuf[slot, t, 2 * g + 1], pbuf[slot, t, 2 * g]], axis=1) for g in range(2)
            ], axis=0)
            right = jnp.concatenate([
                jnp.concatenate([apbuf[ap_index, 1 - g], apbuf[ap_index, 3 - g]], axis=1) for g in range(2)
            ], axis=0)
            out_ref[rows, :] += lax.dot_general(
                left, right, (((0,), (0,)), ((), ())), preferred_element_type=jnp.float32
            )

        return jnp.where(t == 1, digits // 8, digits)

    lax.fori_loop(0, 2 * SLOTS, multiply, digits)
    for_roles(finish)


def on_device(prolong, applied, prolong_pattern, applied_pattern):
    return pl.pallas_call(
        kernel,
        out_shape=jax.ShapeDtypeStruct((prolong.shape[1], applied.shape[1]), jnp.float32),
        in_specs=[
            pl.BlockSpec(memory_space=pl.ANY),
            pl.BlockSpec(memory_space=pl.ANY),
            pl.BlockSpec(memory_space=pl.ANY),
            pl.BlockSpec(memory_space=pl.ANY),
        ],
        out_specs=pl.BlockSpec(memory_space=pltpu.VMEM),
        scratch_shapes=[
            pltpu.VMEM((SLOTS, 2, 4, GROUP, TILE), jnp.bfloat16),
            pltpu.VMEM((2 + SLOTS, 4, GROUP, TILE), jnp.bfloat16),
            pltpu.VMEM((MOST_SLABS, GROUP, TILE), jnp.bfloat16),
            pltpu.SMEM((4, 6), jnp.int32),
            pltpu.SMEM((2, 12), jnp.int32),
            pltpu.SemaphoreType.DMA((18,)),
            pltpu.SemaphoreType.DMA((MOST_SENDS,)),
            pltpu.SemaphoreType.DMA((SLOTS, 4)),
            pltpu.SemaphoreType.DMA((SLOTS, 2)),
            pltpu.SemaphoreType.DMA((MOST_RELAYED,)),
        ],
        compiler_params=pltpu.CompilerParams(
            collective_id=0, has_side_effects=True, vmem_limit_bytes=56000000
        ),
    )(
        prolong,
        applied,
        pltpu.with_memory_space_constraint(prolong_pattern.T, pltpu.HBM),
        pltpu.with_memory_space_constraint(applied_pattern.T, pltpu.HBM),
    )


def solution(mesh):
    in_specs = (P("col", "row"), P("row", "col"), P("col", "row"), P("row", "col"))
    out_specs = P("row", "col")
    return jax.shard_map(
        on_device, mesh=mesh, in_specs=in_specs, out_specs=out_specs, check_vma=False
    )
```

```python
import collections

import jax
import jax.numpy as jnp
from jax import lax
from jax.experimental import pallas as pl
from jax.experimental.pallas import tpu as pltpu
from jax.sharding import PartitionSpec as P

MESH = pl.DeviceIdType.MESH
TILE = 128
ROWS = 8
COLS = 16
GROUP = 384
HALF = 256
FAR = 5
OWN = 2
SLOTS = 6
ORDER = (OWN, 1, 3, 0, 4, FAR)
SOURCE = -1
RELAY = 5
ACROSS = 6
EVERY = frozenset(range(4))

ROUTES = (
    (-1, -1, -1, 0, 1, 0, -1, 62, 87, 337, 250, 54, 229, 42, 19, 180, 176, 166, 0),
    (-1, 1, -1, -1, 1, -1, -1, 412, 396, 367, 103, 329, 21, 245, 74, 154, 230, 162, 0),
    (-1, 1, -1, 4, 1, -1, -1, 255, 406, 307, 281, 163, 335, 261, 114, 231, 254, 62, 0),
    (17, 3, 5, 5, -1, 5, -1, 277, 290, 262, 298, 429, 239, 259, 143, 181, 173, 184, 56),
    (-1, -1, -1, -1, 2, -1, -1, 383, 106, 76, 427, 293, 265, 200, 64, 121, 235, 133, 0),
    (-1, -1, -1, 1, 0, -1, -1, 333, 404, 74, 270, 476, 321, 132, 107, 253, 236, 194, 0),
    (17, -1, 5, 5, 0, 0, -1, 279, 238, 205, 124, 414, 17, 84, 198, 234, 182, 241, 72),
    (19, 3, 5, 5, -1, 5, -1, 154, 269, 351, 157, 343, 16, 155, 147, 118, 37, 152, 30),
    (-1, 2, -1, -1, 2, 1, -1, 49, 374, 33, 446, 449, 219, 213, 159, 85, 219, 258, 0),
    (35, -1, 0, 5, 5, 5, -1, 46, 461, 240, 110, 86, 313, 33, 251, 188, 167, 221, 69),
    (-1, -1, -1, 3, -1, -1, -1, 439, 252, 31, 381, 132, 257, 100, 106, 218, 77, 49, 0),
    (-1, -1, -1, 0, 1, -1, -1, 320, 417, 183, 166, 369, 319, 127, 52, 237, 185, 103, 54),
    (-1, -1, -1, -1, 2, -1, -1, 148, 139, 44, 310, 273, 349, 80, 43, 170, 212, 68, 0),
    (-1, -1, -1, -1, 1, -1, -1, 466, 150, 182, 430, 51, 13, 11, 156, 144, 38, 17, 14),
    (-1, -1, -1, 4, 1, -1, -1, 175, 99, 71, 5, 81, 249, 4, 8, 157, 248, 9, 0),
    (-1, 4, -1, 4, 4, -1, -1, 212, 428, 82, 340, 263, 121, 21, 34, 204, 256, 31, 0),
    (35, -1, -1, 5, 5, -1, -1, 401, 388, 198, 228, 409, 189, 250, 197, 193, 226, 110, 78),
    (-1, -1, -1, 1, 0, -1, -1, 116, 96, 370, 128, 377, 211, 47, 88, 186, 232, 220, 0),
    (-1, -1, 4, 3, -1, -1, -1, 216, 41, 57, 18, 305, 186, 150, 262, 148, 41, 171, 0),
    (-1, -1, -1, 1, 0, -1, -1, 256, 194, 64, 447, 443, 193, 93, 134, 206, 187, 243, 0),
    (3, -1, 5, 0, -1, 5, -1, 236, 12, 363, 469, 168, 248, 86, 214, 203, 172, 223, 61),
    (-1, -1, -1, 1, 1, 1, -1, 356, 387, 197, 20, 174, 1, 246, 104, 233, 209, 217, 0),
    (44, -1, -1, 5, 5, -1, -1, 380, 448, 83, 454, 415, 14, 158, 242, 190, 222, 137, 95),
    (-1, -1, 4, 0, 4, -1, -1, 312, 42, 271, 259, 84, 467, 207, 161, 66, 142, 36, 0),
    (-1, -1, -1, 0, 1, -1, -1, 67, 287, 231, 336, 140, 306, 97, 65, 249, 164, 102, 48),
    (-1, -1, -1, 0, 1, 1, -1, 38, 35, 180, 474, 111, 215, 23, 12, 255, 191, 119, 0),
    (-1, -1, 2, -1, 2, -1, -1, 223, 258, 460, 456, 191, 230, 115, 224, 76, 202, 75, 0),
    (5, 5, -1, 1, 5, -1, -1, 0, 53, 368, 384, 338, 70, 22, 13, 124, 149, 20, 0),
    (-1, -1, 4, -1, 0, -1, -1, 37, 201, 435, 472, 90, 178, 105, 153, 98, 215, 99, 0),
    (53, -1, -1, 0, 5, -1, -1, 288, 437, 272, 346, 458, 420, 139, 91, 141, 184, 32, 0),
    (-1, -1, -1, -1, 2, 0, -1, 142, 24, 28, 123, 105, 324, 125, 140, 94, 189, 247, 0),
    (-1, -1, -1, -1, 2, -1, -1, 296, 190, 379, 113, 275, 426, 79, 57, 238, 174, 101, 87),
    (4, -1, 5, -1, -1, -1, -1, 403, 131, 204, 372, 91, 210, 113, 179, 0, 0, 0, 70),
    (-1, -1, 0, -1, -1, -1, -1, 29, 391, 26, 172, 241, 267, 35, 160, 0, 0, 0, 0),
    (-1, 1, -1, -1, -1, -1, -1, 151, 375, 438, 39, 89, 433, 0, 163, 0, 0, 0, 0),
    (-1, -1, -1, -1, -1, -1, -1, 425, 134, 444, 209, 303, 177, 0, 71, 0, 0, 0, 0),
    (-1, -1, 0, -1, -1, -1, -1, 170, 100, 95, 261, 398, 10, 122, 244, 0, 0, 0, 0),
    (-1, -1, -1, -1, -1, -1, -1, 328, 192, 72, 422, 65, 108, 201, 192, 0, 0, 0, 0),
    (4, -1, 5, -1, -1, -1, -1, 200, 459, 55, 418, 237, 184, 0, 227, 0, 0, 0, 120),
    (-1, 1, -1, -1, -1, -1, -1, 331, 138, 135, 79, 118, 69, 0, 92, 0, 0, 0, 108),
    (12, 5, 5, -1, -1, -1, -1, 441, 300, 278, 440, 78, 207, 126, 178, 0, 0, 0, 53),
    (-1, -1, 0, -1, -1, -1, -1, 220, 243, 264, 45, 232, 11, 168, 205, 0, 0, 0, 16),
    (4, 5, 5, -1, -1, -1, -1, 27, 30, 22, 233, 188, 468, 0, 240, 0, 0, 0, 138),
    (-1, -1, 0, -1, -1, -1, -1, 208, 341, 359, 311, 390, 187, 0, 151, 0, 0, 0, 0),
    (-1, 1, -1, -1, -1, -1, -1, 68, 34, 136, 88, 242, 251, 0, 146, 0, 0, 0, 0),
    (-1, -1, -1, -1, -1, -1, -1, 143, 164, 413, 297, 173, 318, 0, 46, 0, 0, 0, 26),
    (-1, -1, -1, -1, -1, -1, -1, 247, 402, 445, 43, 176, 147, 96, 50, 0, 0, 0, 0),
    (-1, -1, 0, -1, -1, -1, -1, 365, 214, 221, 126, 350, 2, 128, 90, 0, 0, 0, 27),
    (-1, 1, -1, -1, -1, -1, -1, 19, 334, 92, 246, 202, 268, 0, 58, 0, 0, 0, 0),
    (-1, 1, -1, -1, -1, -1, -1, 376, 50, 419, 6, 282, 342, 0, 89, 0, 0, 0, 15),
    (-1, -1, 0, -1, -1, -1, -1, 327, 477, 436, 167, 66, 161, 0, 7, 0, 0, 0, 0),
    (-1, -1, 0, -1, -1, -1, -1, 226, 475, 385, 59, 473, 455, 0, 2, 0, 0, 0, 1),
    (12, 5, 5, -1, -1, -1, -1, 120, 353, 348, 355, 463, 274, 0, 196, 0, 0, 0, 67),
    (4, 5, 5, -1, -1, -1, -1, 141, 332, 107, 308, 291, 283, 0, 145, 0, 0, 0, 28),
    (12, 5, 5, -1, -1, -1, -1, 285, 366, 181, 152, 245, 179, 116, 129, 0, 0, 0, 5),
    (4, 5, 5, -1, -1, -1, -1, 3, 23, 109, 80, 295, 63, 10, 44, 0, 0, 0, 3),
    (57, 5, 5, -1, -1, -1, -1, 117, 206, 149, 462, 345, 304, 0, 252, 0, 0, 0, 136),
    (-1, -1, 0, -1, -1, -1, -1, 130, 235, 7, 326, 434, 125, 0, 117, 0, 0, 0, 0),
    (-1, -1, -1, -1, -1, -1, -1, 471, 330, 48, 452, 155, 389, 229, 208, 0, 0, 0, 0),
    (4, 5, 5, -1, -1, -1, -1, 85, 129, 225, 254, 93, 32, 101, 165, 0, 0, 0, 39),
    (-1, 1, -1, -1, -1, -1, -1, 280, 442, 61, 289, 411, 4, 0, 239, 0, 0, 0, 0),
    (-1, -1, 0, -1, -1, -1, -1, 386, 354, 25, 314, 465, 371, 0, 260, 0, 0, 0, 0),
    (-1, 1, -1, -1, -1, -1, -1, 407, 165, 451, 292, 160, 464, 257, 195, 0, 0, 0, 0),
    (-1, 1, -1, -1, -1, -1, -1, 410, 156, 315, 260, 316, 185, 225, 135, 0, 0, 0, 0),
    (12, -1, 5, -1, -1, -1, -1, 276, 227, 114, 104, 234, 94, 0, 112, 0, 0, 0, 60),
    (-1, -1, -1, -1, -1, -1, -1, 431, 399, 115, 58, 299, 137, 0, 29, 0, 0, 0, 0),
    (-1, -1, -1, -1, -1, -1, -1, 360, 325, 364, 97, 394, 378, 216, 169, 0, 0, 0, 63),
    (-1, -1, 0, -1, -1, -1, -1, 301, 195, 421, 47, 145, 77, 55, 210, 0, 0, 0, 0),
    (-1, -1, 0, -1, -1, -1, -1, 101, 323, 199, 36, 362, 309, 6, 175, 0, 0, 0, 0),
    (-1, 1, -1, -1, -1, -1, -1, 479, 75, 266, 52, 196, 286, 131, 25, 0, 0, 0, 59),
    (-1, 1, -1, -1, -1, -1, -1, 457, 218, 60, 395, 358, 432, 0, 51, 0, 0, 0, 0),
    (-1, 1, -1, -1, -1, -1, -1, 153, 8, 382, 144, 478, 244, 0, 81, 0, 0, 0, 0),
    (-1, -1, -1, -1, -1, -1, -1, 112, 470, 322, 159, 294, 302, 40, 111, 0, 0, 0, 0),
    (-1, -1, 0, -1, -1, -1, -1, 416, 224, 217, 213, 127, 146, 73, 123, 0, 0, 0, 18),
    (-1, -1, -1, -1, -1, -1, -1, 339, 453, 397, 361, 222, 317, 211, 109, 0, 0, 0, 24),
    (-1, -1, 0, -1, -1, -1, -1, 9, 73, 171, 344, 56, 98, 83, 45, 0, 0, 0, 0),
    (-1, 1, -1, -1, -1, -1, -1, 162, 102, 253, 400, 169, 133, 228, 82, 0, 0, 0, 0),
    (-1, -1, -1, -1, -1, -1, -1, 284, 405, 450, 40, 424, 203, 183, 177, 0, 0, 0, 0),
    (-1, -1, 0, -1, -1, -1, -1, 158, 122, 408, 357, 119, 423, 0, 130, 0, 0, 0, 0),
    (-1, -1, -1, -1, -1, -1, -1, 393, 347, 392, 15, 352, 373, 0, 199, 0, 0, 0, 0),
)


def chip_of(device):
    return device[1] // 4, device[0] // 2, device[1] % 4


def role_of(device):
    x, y, z = chip_of(device)
    return (x - y) % 4, z, device[0] % 2


def p_kind(r, cp):
    m, h = cp // 2, cp % 2
    if m == r:
        return 0
    if (m == r + 1 and h == 0) or (m == r - 1 and h == 1):
        return 1
    return 2 if m == (r + 4) % ROWS else None


def p_pieces(kind, h):
    if kind == 0:
        return ((h, 0, 2, 0), (h, 2, 2, 1), (1 - h, 1 - h, 2, 2), (1 - h, 3 - h, 1, 3))
    half, start = (1 - h, h) if kind == 1 else (h, 0)
    return ((half, start, 2, 2), (half, start + 2, 1, 3))


def ap_pieces(slot):
    if slot == 4:
        return ((1, 2, 0), (3, 1, 1))
    return ((0, 2, 0), (2, 1 if slot in (0, FAR) else 2, 1))


def pieces():
    found = collections.OrderedDict()
    for r in range(ROWS):
        for cp in range(COLS):
            kind = p_kind(r, cp)
            if kind is None:
                continue
            z = cp % 4
            for n, (half, at, size, piece) in enumerate(p_pieces(kind, z % 2)):
                users = {n: (r, cp + d) for n, d in enumerate((-1, 1, -2, 2)) if 0 <= cp + d < COLS}
                users[4] = (r, (cp + 8) % COLS)
                entry = found.setdefault((0, kind, z, n), ((half, at, size, piece), []))
                entry[1].append(((r, cp), users))
    for r in range(ROWS):
        for c in range(COLS):
            for half in range(2):
                v = 2 * r + half - c
                slot = v + 2 if -2 <= v <= 2 else FAR if v in (8, -8) else None
                if slot is None:
                    continue
                x, y, z = chip_of((r, c))
                side = r - 1 + 2 * half
                for n, (at, size, piece) in enumerate(ap_pieces(slot)):
                    users = {1: ((r + 4) % ROWS, c)}
                    if 0 <= side < ROWS:
                        users[0 if side // 2 != r // 2 else ACROSS] = (side, c)
                    key = (1, r % 2, half, (x - y) % 4, z, n)
                    entry = found.setdefault(key, ((slot, half, at, size, piece), []))
                    entry[1].append(((r, c), users))
    return found


P_SLOT = (3, 1, 4, 0, FAR)

class Role:
    def __init__(self):
        self.sends = {}
        self.arrivals = {}
        self.greets = {}
        self.partners = {y: set() for y in range(4)}
        self.relayed = {}
        self.slabs = 0


def move_between(a, b):
    (ax, ay, _), (bx, by, bz) = chip_of(a), chip_of(b)
    return (bx - ax) % 4, (by - ay) % 4, bz, b[0] % 2


def make_plan():
    roles = {(a, z, core): Role() for a in range(4) for z in range(4) for core in range(2)}
    kinds = list(pieces().items())
    for n, (key, (_, instances)) in enumerate(kinds):
        size = kinds[n][1][0][3] if key[0] else kinds[n][1][0][2]
        offset, parents = ROUTES[n][0], ROUTES[n][1:7]
        for source, users in instances:
            place = dict(users)
            x, y, z = chip_of(source)
            if offset >= 0:
                rx, ry, rz = (x + offset % 4) % 4, (y + offset // 4 % 4) % 4, (z + offset // 16) % 4
                place[RELAY] = (2 * ry + source[0] % 2, 4 * rx + rz)
            place[SOURCE] = source
            reached = {SOURCE: SOURCE}
            edges = []

            def reach(node):
                if node in reached:
                    return reached[node]
                up = SOURCE if node == ACROSS else parents[node]
                if node not in place:
                    reached[node] = reach(up)
                    return reached[node]
                same = [u for u in users if node == RELAY and users[u] == place[RELAY]]
                if node == RELAY and place[RELAY] == source:
                    reached[node] = SOURCE
                    return SOURCE
                if same:
                    reached[same[0]] = same[0]
                    reached[node] = same[0]
                    edges.append((reach(up), same[0]))
                    return same[0]
                reached[node] = node
                edges.append((reach(up), node))
                return node

            if RELAY in place and RELAY in [parents[u] for u in users if u != ACROSS]:
                reach(RELAY)
            for user in users:
                reach(user)
            for a, b in edges:
                here, there = place[a], place[b]
                assert here != there
                mine, theirs = roles[role_of(here)], roles[role_of(there)]
                edge = (n, a, b, move_between(here, there))
                mine.sends.setdefault(edge, set()).add(here[0] // 2)
                theirs.arrivals.setdefault((n, b), set()).add(there[0] // 2)
                theirs.greets.setdefault(move_between(there, here), set()).add(there[0] // 2)
                mine.partners[here[0] // 2].add(there)
                if b == RELAY and n not in theirs.relayed:
                    theirs.relayed[n] = (theirs.slabs, len(theirs.relayed))
                    theirs.slabs += size
    return kinds, roles


KINDS, PLAN = make_plan()
MOST_SENDS = max(len(role.sends) for role in PLAN.values())
MOST_SLABS = max(max(role.slabs for role in PLAN.values()), 1)
MOST_RELAYED = max(max(len(role.relayed) for role in PLAN.values()), 1)


def target_role(role, move):
    return (role[0] + move[0] - move[1]) % 4, move[2], move[3]


def time_of(n, node):
    return -1 if node == ACROSS else ROUTES[n][13 + node]


def order_of_slots(role, member):
    latest = {slot: -1 for slot in ORDER}
    for (kind, node), members in PLAN[role].arrivals.items():
        if member in members and node != RELAY:
            key, (shape, _) = KINDS[kind]
            slot = shape[0] if key[0] else P_SLOT[node]
            latest[slot] = max(latest[slot], time_of(kind, node))
    return sum(slot * 8**n for n, slot in enumerate(sorted(ORDER, key=lambda slot: latest[slot])))


DIGITS = {(r, c): order_of_slots(role_of((r, c)), r // 2) for r in range(ROWS) for c in range(COLS)}


def column_of(c, slot):
    near = c + slot - 2
    far = slot == FAR
    cp = jnp.where(far, (c + 8) % COLS, near)
    return cp, far | ((near >= 0) & (near < COLS))


def shape_of(r, cp):
    m, h = cp // 2, cp % 2
    main = m == r
    low = (m == r + 1) & (h == 0)
    high = (m == r - 1) & (h == 1)
    far = m == (r + 4) % ROWS
    any3 = main | low | high | far
    half3 = jnp.where(far, h, 1 - h)
    start3 = jnp.where(main, 1 - h, jnp.where(high, 1, 0))
    return main, any3, half3, start3


def kernel(p_hbm, ap_hbm, pp_hbm, app_hbm, out_ref, pbuf, apbuf, relaybuf, pp_ref, app_ref,
           load_sem, send_sem, precv, aprecv, relayrecv):
    r = lax.axis_index("row")
    c = lax.axis_index("col")
    x, y, z, core = c // 4, r // 2, c % 4, r % 2
    diagonal = (x - y + 4) % 4
    is_y = [y == n for n in range(4)]

    def for_members(members, act):
        if members == EVERY:
            act()
        elif members:
            test = None
            for n in sorted(members):
                test = is_y[n] if test is None else test | is_y[n]
            pl.when(test)(act)

    def for_roles(act):
        def for_z(a):
            for zz in range(4):
                def for_core(zz=zz):
                    for cc in range(2):
                        pl.when(core == cc)(lambda cc=cc: act((a, zz, cc)))
                pl.when(z == zz)(for_core)
        for a in range(4):
            pl.when(diagonal == a)(lambda a=a: for_z(a))

    def device(move):
        return 2 * ((y + move[1]) % 4) + move[3], 4 * ((x + move[0]) % 4) + move[2]

    def region(n, node, role):
        key, (shape, _) = KINDS[n]
        if node == RELAY:
            first, index = PLAN[role].relayed[n]
            size = shape[3] if key[0] else shape[2]
            return relaybuf.at[pl.ds(first, size)], relayrecv.at[index]
        if key[0] == 0:
            half, at, size, piece = shape
            slot = OWN if node == SOURCE else P_SLOT[node]
            return pbuf.at[slot, half, pl.ds(at, size)], precv.at[slot, piece]
        slot, half, at, size, piece = shape
        return apbuf.at[half if node == SOURCE else 2 + slot, pl.ds(at, size)], aprecv.at[slot, piece]

    def copy_of(role, edge):
        n, a, b, move = edge
        source, _ = region(n, a, role)
        target, recv = region(n, b, target_role(role, move))
        return pltpu.make_async_remote_copy(
            src_ref=source,
            dst_ref=target,
            send_sem=send_sem.at[list(PLAN[role].sends).index(edge)],
            recv_sem=recv,
            device_id=device(move),
            device_id_type=MESH,
        )

    def arrived(role, n, node):
        target, recv = region(n, node, role)
        pltpu.make_async_remote_copy(
            src_ref=target, dst_ref=target, send_sem=send_sem.at[0], recv_sem=recv,
            device_id=(r, c), device_id_type=MESH,
        ).wait_recv()

    def order_of(edge):
        n, _, b, _ = edge
        return -1 if b == ACROSS else ROUTES[n][7 + b]

    def passed_on(role):
        found = {}
        for (n, a, _, _), members in PLAN[role].sends.items():
            if a != SOURCE:
                found.setdefault((n, a), set()).update(members)
        return found

    barrier = pltpu.get_barrier_semaphore()

    def greet(role):
        for move, members in sorted(PLAN[role].greets.items()):
            for_members(members, lambda move=move: pl.semaphore_signal(
                barrier, inc=1, device_id=device(move), device_id_type=MESH))

    def send(role):
        plan = PLAN[role]
        counts = {}
        for n, partners in plan.partners.items():
            counts.setdefault(len(partners), set()).add(n)
        for count, members in counts.items():
            if count:
                for_members(members, lambda count=count: pl.semaphore_wait(barrier, count))
        for edge in sorted((e for e in plan.sends if e[1] == SOURCE), key=order_of):
            for_members(plan.sends[edge], lambda edge=edge: copy_of(role, edge).start())

    def pass_on(role):
        plan = PLAN[role]
        waits = sorted(passed_on(role).items(), key=lambda item: time_of(*item[0]))
        for (n, node), members in waits:
            for_members(members, lambda n=n, node=node: arrived(role, n, node))
            for edge in sorted((e for e in plan.sends if e[:2] == (n, node)), key=order_of):
                for_members(plan.sends[edge], lambda edge=edge: copy_of(role, edge).start())

    def finish(role):
        for edge, members in PLAN[role].sends.items():
            for_members(members, lambda edge=edge: copy_of(role, edge).wait_send())

    def await_step(step):
        def one(role):
            handed = passed_on(role)
            by_step = {}
            for (n, node), members in PLAN[role].arrivals.items():
                left = members - handed.get((n, node), set())
                if node == RELAY or not left:
                    continue
                key, (shape, _) = KINDS[n]
                at = 2 * shape[0] if key[0] else 2 * P_SLOT[node] + shape[0]
                by_step.setdefault(at, []).append((n, node, left))
            for at, waits in sorted(by_step.items()):
                @pl.when(step == at)
                def _():
                    for n, node, left in waits:
                        for_members(left, lambda n=n, node=node: arrived(role, n, node))

        for_roles(one)

    for_roles(greet)

    loads = []
    for g in range(2):
        for i in range(4):
            loads.append(pltpu.make_async_copy(
                p_hbm.at[pl.ds(g * GROUP, GROUP), pl.ds(i * TILE, TILE)],
                pbuf.at[OWN, i // 2, 2 * g + 1 - i % 2],
                load_sem.at[4 * g + i],
            ))
    for q in range(4):
        for j in range(2):
            loads.append(pltpu.make_async_copy(
                ap_hbm.at[pl.ds(q * GROUP, GROUP), pl.ds(j * TILE, TILE)],
                apbuf.at[q // 2, 2 * j + 1 - q % 2],
                load_sem.at[8 + 2 * q + j],
            ))
    loads.append(pltpu.make_async_copy(pp_hbm, pp_ref, load_sem.at[16]))
    loads.append(pltpu.make_async_copy(app_hbm, app_ref, load_sem.at[17]))
    for load in loads:
        load.start()
    for load in loads:
        load.wait()
    for a in range(6):
        g, rows = a // 3, pl.ds(a % 3 * TILE, TILE)
        for i in range(4):
            weight = pp_ref[i, a].astype(jnp.float32).astype(jnp.bfloat16)
            slab = (OWN, i // 2, 2 * g + 1 - i % 2, rows)
            pbuf[slab] = pbuf[slab] * weight
    for a in range(12):
        q, rows = a // 3, pl.ds(a % 3 * TILE, TILE)
        for j in range(2):
            weight = app_ref[j, a].astype(jnp.float32).astype(jnp.bfloat16)
            slab = (q // 2, 2 * j + 1 - q % 2, rows)
            apbuf[slab] = apbuf[slab] * weight

    for_roles(send)

    blank = jnp.zeros((GROUP, TILE), jnp.bfloat16)
    apbuf[2 + 0, 3] = blank
    apbuf[2 + 4, 0] = blank
    apbuf[2 + FAR, 3] = blank
    for slot in range(SLOTS):
        if slot != OWN:
            cp, ok = column_of(c, slot)
            _, any3, half, start = shape_of(r, cp)

            @pl.when(ok & any3)
            def _():
                pbuf[slot, half, jnp.where(start == 0, 3, 0)] = blank
    out_ref[...] = jnp.zeros_like(out_ref)

    def add_product(slot, t, ap_index):
        rows = pl.ds(pl.multiple_of(t * HALF, HALF), HALF)
        left = jnp.concatenate([
            jnp.concatenate([pbuf[slot, t, 2 * g + 1], pbuf[slot, t, 2 * g]], axis=1) for g in range(2)
        ], axis=0)
        right = jnp.concatenate([
            jnp.concatenate([apbuf[ap_index, 1 - g], apbuf[ap_index, 3 - g]], axis=1) for g in range(2)
        ], axis=0)
        out_ref[rows, :] += lax.dot_general(
            left, right, (((0,), (0,)), ((), ())), preferred_element_type=jnp.float32
        )

    own_first = c // 2 == r

    @pl.when(own_first)
    def _():
        def one(t, carry):
            add_product(OWN, t, c % 2)
            return carry

        lax.fori_loop(0, 2, one, 0)

    for_roles(pass_on)

    number = r * COLS + c
    usual = collections.Counter(DIGITS.values()).most_common(1)[0][0]
    digits = jnp.int32(usual)
    for (row, col), order in DIGITS.items():
        if order != usual:
            digits = jnp.where(number == row * COLS + col, order, digits)

    def multiply(step, digits):
        t = step % 2
        slot = digits % 8
        cp, ok = column_of(c, slot)
        main, any3, half3, _ = shape_of(r, cp)
        m, h = cp // 2, cp % 2
        full = main & (t == h)
        part = any3 & (t == half3)
        await_step(2 * slot + t)

        @pl.when(ok & (full | part) & jnp.logical_not(own_first & (slot == OWN)))
        def _():
            add_product(slot, t, jnp.where(m == r, h, 2 + slot))

        return jnp.where(t == 1, digits // 8, digits)

    lax.fori_loop(0, 2 * SLOTS, multiply, digits)
    for_roles(finish)


def on_device(prolong, applied, prolong_pattern, applied_pattern):
    return pl.pallas_call(
        kernel,
        out_shape=jax.ShapeDtypeStruct((prolong.shape[1], applied.shape[1]), jnp.float32),
        in_specs=[
            pl.BlockSpec(memory_space=pl.ANY),
            pl.BlockSpec(memory_space=pl.ANY),
            pl.BlockSpec(memory_space=pl.ANY),
            pl.BlockSpec(memory_space=pl.ANY),
        ],
        out_specs=pl.BlockSpec(memory_space=pltpu.VMEM),
        scratch_shapes=[
            pltpu.VMEM((SLOTS, 2, 4, GROUP, TILE), jnp.bfloat16),
            pltpu.VMEM((2 + SLOTS, 4, GROUP, TILE), jnp.bfloat16),
            pltpu.VMEM((MOST_SLABS, GROUP, TILE), jnp.bfloat16),
            pltpu.SMEM((4, 6), jnp.int32),
            pltpu.SMEM((2, 12), jnp.int32),
            pltpu.SemaphoreType.DMA((18,)),
            pltpu.SemaphoreType.DMA((MOST_SENDS,)),
            pltpu.SemaphoreType.DMA((SLOTS, 4)),
            pltpu.SemaphoreType.DMA((SLOTS, 2)),
            pltpu.SemaphoreType.DMA((MOST_RELAYED,)),
        ],
        compiler_params=pltpu.CompilerParams(
            collective_id=0, has_side_effects=True, vmem_limit_bytes=56000000
        ),
    )(
        prolong,
        applied,
        pltpu.with_memory_space_constraint(prolong_pattern.T, pltpu.HBM),
        pltpu.with_memory_space_constraint(applied_pattern.T, pltpu.HBM),
    )


def solution(mesh):
    in_specs = (P("col", "row"), P("row", "col"), P("col", "row"), P("row", "col"))
    out_specs = P("row", "col")
    return jax.shard_map(
        on_device, mesh=mesh, in_specs=in_specs, out_specs=out_specs, check_vma=False
    )
```
